32 devices in a mesh: dp: 4 (over y, core), label: 8 (over z, x).
Axes of the slice: x: 2, y: 2, z: 4, core: 2. Of those that a mesh axis runs over, the one named last changes fastest.
Arguments:
- calib: bfloat16 [16384, 2688], P(('dp', 'label')), may hold values from -160 to 160
- block_weight: bfloat16 [8192, 128], P('dp', 'label'), may hold values from -0.125 to 0.125
- rest_weight: bfloat16 [8192, 2560], P('dp', 'label'), may hold values from -0.125 to 0.125
- prune_mask: int32 [8192, 128], P(('dp', 'label')), may hold values 0 or 1
Outputs:
- pruned_block: bfloat16 [8192, 128], P(('dp', 'label'))
- updated_rest: bfloat16 [8192, 2560], P('dp', 'label')
The draws below stay inside these ranges and needn't reach their ends.
All inputs are finite; a program needn't handle non-finite values. No bound on the sum of `prune_mask` on one device may be relied on, other than what follows from the above.
Results may differ from the reference program's by a relative error of at most 0.00075.
Values may be sent and summed in bfloat16 or wider, within the bound.
A program may use at most 64 MiB of HBM per device.

```python
import math
import jax
import jax.numpy as jnp
from jax import lax

DH = 2688
BLOCK = 128
ITERS = 6
NCAL = 16384
VOCAB = 8192


def draw_calib(key, part):
    key_scale = jax.random.fold_in(key, 11)
    key_base = jax.random.fold_in(key, 12)
    column_scale = jnp.exp(jax.random.uniform(key_scale, (DH,), jnp.float32, 0.0, math.log(10.0)))
    position = jnp.arange(NCAL, dtype=jnp.float32)[:, None] / (NCAL - 1)
    ramp = jnp.exp(math.log(2.5) * position)
    noise = jnp.clip(jax.random.normal(key_base, (NCAL, DH), jnp.float32), -6.0, 6.0)
    mixed = noise + 0.3 * jnp.roll(noise, 1, axis=1) + 0.15 * jnp.roll(noise, 7, axis=1)
    return (mixed * ramp * column_scale[None, :] * 0.6).astype(jnp.bfloat16)


def set_ends(entries, own_key, low, top_value):
    longest = entries.shape.index(max(entries.shape))
    spots = []
    for shift in (0, 1):
        where = [jax.random.randint(jax.random.fold_in(own_key, axis), (), 0, length) for axis, length in enumerate(entries.shape)]
        where[longest] = (where[longest] + shift) % entries.shape[longest]
        spots.append(tuple(where))
    return entries.at[spots[0]].set(low).at[spots[1]].set(top_value)


def level_of(stream_key, shape, shards, smallest, top_value):
    loudness = 1.0
    for dim, parts in shards:
        steps = jax.random.uniform(jax.random.fold_in(jax.random.fold_in(stream_key, 6), dim), (parts,), jnp.float32, smallest / len(shards), top_value / len(shards))
        loudness = loudness * jnp.repeat(jnp.exp(steps), shape[dim] // parts).reshape((-1,) + (1,) * (len(shape) - 1 - dim))
    return loudness


def normal_values(own_key, shape, scale, bound, split=(), held_as=jnp.bfloat16):
    values = scale * jax.random.normal(own_key, shape, jnp.float32)
    if split:
        values = values * level_of(own_key, shape, split, -0.22, 0.18)
    return jnp.clip(values, -bound, bound).astype(held_as)


def setup_inputs(seed: int = 0) -> dict:
    streams_of = jax.random.split(jax.random.key(seed), 5)
    return {
        "calib": draw_calib(jax.random.fold_in(streams_of[4], 71), 0),
        "block_weight": normal_values(streams_of[1], (VOCAB, BLOCK), DH ** -0.5, 0.125, ((0, 4), (1, 8))),
        "rest_weight": normal_values(streams_of[2], (VOCAB, DH - BLOCK), DH ** -0.5, 0.125, ((0, 4), (1, 8))),
        "prune_mask": set_ends((jax.random.randint(streams_of[3], (VOCAB, BLOCK), 0, 2) < 1).astype(jnp.int32), jax.random.fold_in(streams_of[3], 1), 0, 1),
    }


damp_fraction = 0.01

def prune_rows(weights, mask, upper):
    maskf = mask.astype(jnp.float32)
    width = weights.shape[1]

    def advance(index, carry):
        current, kept, errors = carry
        column = lax.dynamic_slice_in_dim(current, index, 1, 1)[:, 0]
        chosen = lax.dynamic_slice_in_dim(maskf, index, 1, 1)[:, 0]
        pivot = lax.dynamic_slice_in_dim(upper, index, 1, 0)[0]
        diagonal = lax.dynamic_index_in_dim(pivot, index, keepdims=False)
        error = chosen * column / diagonal
        kept = lax.dynamic_update_slice_in_dim(kept, ((1.0 - chosen) * column)[:, None], index, 1)
        errors = lax.dynamic_update_slice_in_dim(errors, error[:, None], index, 1)
        current = current - error[:, None] * pivot[None, :]
        return (current, kept, errors)
    start = (weights.astype(jnp.float32), jnp.zeros(weights.shape, jnp.float32), jnp.zeros(weights.shape, jnp.float32))
    result = lax.fori_loop(0, width, advance, start)
    return (result[1], result[2])

def reference(calib, block_weight, rest_weight, prune_mask):
    total = calib.shape[0]
    width = calib.shape[1]
    block = block_weight.shape[1]
    colsq = jnp.sum(jnp.square(calib.astype(jnp.float32)), axis=0)
    damping = damp_fraction * 2.0 * jnp.sum(colsq) / (total * width)
    scale = 2.0 / total
    hdiag = (scale * colsq + damping)[:, None]
    resid = jnp.eye(width, block, dtype=jnp.float32)
    precond = resid / hdiag
    direction = precond
    solution = jnp.zeros((width, block), jnp.float32)
    rho = jnp.sum(resid * precond, axis=0)
    for step in range(ITERS):
        inner = jnp.einsum('tk,kb->tb', calib.astype(jnp.float32), direction.astype(jnp.float32), precision=lax.Precision.HIGHEST, preferred_element_type=jnp.float32)
        outer = jnp.einsum('tk,tb->kb', calib.astype(jnp.float32), inner.astype(jnp.float32), precision=lax.Precision.HIGHEST, preferred_element_type=jnp.float32)
        image = scale * outer + damping * direction
        alpha = rho / jnp.sum(direction * image, axis=0)
        solution = solution + alpha * direction
        resid = resid - alpha * image
        precond = resid / hdiag
        fresh = jnp.sum(resid * precond, axis=0)
        direction = precond + fresh / rho * direction
        rho = fresh
    top = 0.5 * (solution[:block] + solution[:block].T)
    lower = jnp.linalg.cholesky(top)
    upper = lower.T
    cross = jax.scipy.linalg.solve_triangular(lower, solution[block:].T, lower=True)
    kept, errors = prune_rows(block_weight, prune_mask, upper)
    delta = jnp.dot(errors.astype(jnp.float32), cross.astype(jnp.float32), precision=lax.Precision.HIGHEST, preferred_element_type=jnp.float32)
    updated = (rest_weight.astype(jnp.float32) - delta).astype(jnp.bfloat16)
    return (kept.astype(jnp.bfloat16), updated)
```

```python
import functools
import math

import jax
import jax.numpy as jnp
from jax import lax
from jax.experimental import pallas as pl
from jax.experimental.pallas import tpu as pltpu
from jax.sharding import PartitionSpec as P

ITERS = 6
MESH = pl.DeviceIdType.MESH

damp_fraction = 0.01
sub_width = 16
CHUNKS = 3
MEMBERS = 8


def two_terms(x):
    high = x.astype(jnp.bfloat16)
    low = (x - high.astype(jnp.float32)).astype(jnp.bfloat16)
    return jnp.concatenate([high, low], axis=0)


def loop(low, high, body):
    def step(d, carry):
        body(d)
        return carry

    lax.fori_loop(low, high, step, 0)


def remote(src, dst, send, recv, to):
    return pltpu.make_async_remote_copy(
        src_ref=src, dst_ref=dst, send_sem=send, recv_sem=recv, device_id=to, device_id_type=MESH
    )


def window_start(label, block, cols, window, width):
    return jnp.minimum((block + label * cols) // 128, (width - window) // 128) * 128


def window_width(block, cols, nl):
    return max(-(-((block + at * cols) % 128 + cols) // 128) * 128 for at in range(nl))


def place(nd, nl):
    nx = math.isqrt(nl // 2)
    ny, nz = nd // 2, nl // nx
    groups = (nx // 2) * (ny // 2) * (nz // 2)
    dp = lax.axis_index("dp")
    label = lax.axis_index("label")
    core, y, z, x = lax.rem(dp, 2), dp // 2, label // nx, lax.rem(label, nx)
    mx, my, mz = lax.rem(x, 2), lax.rem(y, 2), lax.rem(z, 2)
    qx, qy, qz = x // 2, y // 2, z // 2
    group = (qz * (ny // 2) + qy) * (nx // 2) + qx

    def member(e):
        hx, hy, hz = lax.rem(mx + lax.rem(e, 2), 2), lax.rem(my + lax.rem(e // 2, 2), 2), lax.rem(mz + e // 4, 2)
        return ((qy * 2 + hy) * 2 + core, (qz * 2 + hz) * nx + qx * 2 + hx), hz * 4 + hy * 2 + hx

    def other(h):
        q = lax.rem(group + h, groups)
        hx, hy, hz = lax.rem(q, nx // 2), lax.rem(q // (nx // 2), ny // 2), q // ((nx // 2) * (ny // 2))
        return ((hy * 2 + my) * 2 + core, (hz * 2 + mz) * nx + hx * 2 + mx)

    partner = (dp + 1 - 2 * core, label)
    return core, mz * 4 + my * 2 + mx, group, groups, member, other, partner


def cg_kernel(
    nd, nl, cols, tokens, c_ref, w_ref, m_ref, top_ref, win_ref, wg_ref, mg_ref,
    x_ref, pbuf, sbuf, rbuf, stbuf, vb, ab, img, xs, rs, ds, inv, damp_ref, diag_ref, rho_ref,
    cz, inner, stat, gs, gb, local_ref, part, slots,
    pair_s, pair_r, rs_s, rs_r, st_s, st_r, ag_s, ag_r, fw_s, fw_r, ab_s, ab_r, abf_s, abf_r,
    sp_s, sp_r, sm_s, sm_r, sg_s, sg_r, g_s, g_r, gf_s, gf_r, e_s, e_r, en_s, en_r, wsend, wrecv, msend, mrecv,
):
    block = top_ref.shape[0]
    width = c_ref.shape[1]
    window = win_ref.shape[1]
    chunk = width // CHUNKS
    half = block // 2
    peers = MEMBERS - 1
    stat_rows = width // 128
    steps = ITERS - 1
    f32 = jnp.float32
    scale = 2.0 / tokens
    core, me, group, groups, member, other, partner = place(nd, nl)
    dp = lax.axis_index("dp")
    label = lax.axis_index("label")
    n = (nd // 2) * nl
    chip = (dp // 2) * nl + label
    own = m_ref.shape[1]

    def lanes(c):
        return pl.ds(c * chunk, chunk)

    def rows8(core_, g):
        return pl.ds(pl.multiple_of(core_ * half + g * 8, 8), 8)

    def rows16(core_, g):
        return pl.ds(pl.multiple_of(core_ * 2 * half + g * 16, 16), 16)

    half_rows = pl.ds(pl.multiple_of(core * half, half), half)
    away_rows = pl.ds(pl.multiple_of((1 - core) * half, half), half)
    half_rows16 = pl.ds(pl.multiple_of(core * 2 * half, 2 * half), 2 * half)
    mine = rows8(core, me)

    def chip_device(d):
        j = lax.rem(chip + d, n)
        return (2 * (j // nl) + core, lax.rem(j, nl))

    def columns(at):
        return (slice(None), pl.ds(pl.multiple_of(at * own, 128), own))

    def beside(e, arriving):
        to = lax.rem(label + (nl - e if arriving else e), nl)
        at = to if arriving else label
        return (
            remote(w_ref, wg_ref.at[at], wsend.at[e], wrecv.at[e], (dp, to)),
            remote(m_ref, mg_ref.at[columns(at)], msend.at[e], mrecv.at[e], (dp, to)),
        )

    def pair(c):
        return remote(x_ref.at[c, away_rows], pbuf.at[c], pair_s.at[c], pair_r.at[c], partner)

    def forward(c):
        ref = vb.at[c, half_rows16]
        return remote(ref, ref, fw_s.at[c], fw_r.at[c], partner)

    def forward_ab():
        ref = ab.at[half_rows]
        return remote(ref, ref, abf_s, abf_r, partner)

    def total_wait(ref, send, recv):
        return remote(ref, ref, send, recv, partner)

    barrier = pltpu.get_barrier_semaphore()
    pl.semaphore_signal(barrier, inc=1, device_id=partner, device_id_type=MESH)
    loop(1, n, lambda d: pl.semaphore_signal(barrier, inc=1, device_id=chip_device(d), device_id_type=MESH))

    def product(lhs, terms, c):
        out = jnp.dot(lhs, c_ref[:, lanes(c)], preferred_element_type=f32)
        x_ref[c] = out[:block] + out[block:] if terms == 2 else out

    def scatter(c):
        pair(c).wait_recv()

        def send(d):
            e = MEMBERS - 1 - d
            to, g = member(e)
            sbuf[c, e] = x_ref[c, rows8(core, g)] + pbuf[c, pl.ds(pl.multiple_of(g * 8, 8), 8)]
            remote(sbuf.at[c, e], rbuf.at[c, e], rs_s.at[c], rs_r.at[c], to).start()

        loop(0, peers, send)

    def cross(c, par):
        acc = x_ref[c, mine] + pbuf[c, pl.ds(pl.multiple_of(me * 8, 8), 8)]
        total_wait(rbuf.at[c, pl.ds(1, peers)], rs_s.at[c], rs_r.at[c]).wait_recv()
        for e in range(1, MEMBERS):
            acc = acc + rbuf[c, e]
        stbuf[par, c, group] = acc
        ref = stbuf.at[par, c, group]
        loop(1, groups, lambda h: remote(ref, ref, st_s.at[par, c], st_r.at[par, c], other(h)).start())

    def crossed(c, par, first):
        if groups > 1:
            total_wait(stbuf.at[par, c, pl.ds(0, groups - 1)], st_s.at[par, c], st_r.at[par, c]).wait_recv()
        acc = stbuf[par, c, 0]
        for h in range(1, groups):
            acc = acc + stbuf[par, c, h]
        if first:
            acc = acc / diag_ref[...]
        direction = ds[:, lanes(c)]
        image = scale * acc + damp_ref[0:8, 0:1] * direction
        img[:, lanes(c)] = image
        vb[c, rows16(core, me)] = two_terms(image * inv[:, lanes(c)])

        def send(d):
            to, g = member(MEMBERS - 1 - d)
            ref = vb.at[c, rows16(core, me)]
            remote(ref, ref, ag_s.at[c], ag_r.at[c], to).start()

        loop(0, peers, send)
        return jnp.sum(direction * image, axis=1, keepdims=True)

    def rescale(curve):
        rho = rho_ref[:, 0:1]
        alpha = rho / curve
        fresh = jnp.zeros((8, 1), f32)
        for c in range(CHUNKS):
            resid = rs[:, lanes(c)] - alpha * img[:, lanes(c)]
            rs[:, lanes(c)] = resid
            fresh = fresh + jnp.sum(resid * resid * inv[:, lanes(c)], axis=1, keepdims=True)
        beta = fresh / rho
        lane = lax.broadcasted_iota(jnp.int32, (8, 128), 1)
        ab[mine] = jnp.where(lane < 64, alpha, beta)

        def send(d):
            to, g = member(MEMBERS - 1 - d)
            remote(ab.at[mine], ab.at[mine], ab_s, ab_r, to).start()

        loop(0, peers, send)
        rho_ref[...] = jnp.broadcast_to(fresh, (8, 128))
        for c in range(CHUNKS):
            direction = ds[:, lanes(c)]
            xs[:, lanes(c)] = xs[:, lanes(c)] + alpha * direction
            ds[:, lanes(c)] = rs[:, lanes(c)] * inv[:, lanes(c)] + beta * direction

    def gather(c):
        total_wait(vb.at[c, pl.ds(0, peers * 16)], ag_s.at[c], ag_r.at[c]).wait_recv()
        forward(c).start()

    def applied(c):
        forward(c).wait_recv()
        return lax.dot_general(
            vb[c], c_ref[:, lanes(c)], (((1,), (1,)), ((), ())), preferred_element_type=f32
        )

    def finish_sends():
        for c in range(CHUNKS):
            total_wait(vb.at[c, pl.ds(0, peers * 16)], ag_s.at[c], ag_r.at[c]).wait_send()
            forward(c).wait_send()
        total_wait(ab.at[pl.ds(0, peers * 8)], ab_s, ab_r).wait_send()
        forward_ab().wait_send()

    def reduce_and_apply(par, first):
        for c in range(CHUNKS):
            scatter(c)
        if first:
            share_stats()
        for c in range(CHUNKS):
            cross(c, par)
        for c in range(CHUNKS):
            pair(c).wait_send()
            total_wait(sbuf.at[c, pl.ds(1, peers)], rs_s.at[c], rs_r.at[c]).wait_send()
        if first:
            start_state()
        curve = jnp.zeros((8, 1), f32)
        for c in range(CHUNKS):
            curve = curve + crossed(c, par, first)
        rescale(curve)
        for c in range(CHUNKS):
            gather(c)
        total_wait(ab.at[pl.ds(0, peers * 8)], ab_s, ab_r).wait_recv()
        forward_ab().start()
        if groups > 1:
            for c in range(CHUNKS):
                total_wait(stbuf.at[par, c, pl.ds(0, groups - 1)], st_s.at[par, c], st_r.at[par, c]).wait_send()
        out = applied(0)
        for c in range(1, CHUNKS):
            out = out + applied(c)
        forward_ab().wait_recv()
        out = out.reshape(2 * block // 16, 2, 8, out.shape[1])
        out = (out[:, 0] + out[:, 1]).reshape(block, out.shape[3])
        applied_z = cz[...] - ab[:, 0:1] * out
        cz[...] = applied_z
        inner[...] = applied_z + ab[:, 64:65] * inner[...]

    local_stat, near_stat, member_stat, group_stat = 0, 1, 2, 2 + MEMBERS

    def pair_stats():
        return remote(stat.at[local_stat], stat.at[near_stat], sp_s, sp_r, partner)

    def share_stats():
        pair_stats().wait_recv()
        stat[member_stat + me] = stat[local_stat] + stat[near_stat]
        ref = stat.at[member_stat + me]
        loop(1, MEMBERS, lambda e: remote(ref, ref, sm_s, sm_r, member(e)[0]).start())

    def start_state():
        total_wait(stat.at[pl.ds(member_stat, peers)], sm_s, sm_r).wait_recv()
        acc = stat[member_stat]
        for e in range(1, MEMBERS):
            acc = acc + stat[member_stat + e]
        stat[group_stat + group] = acc
        ref = stat.at[group_stat + group]
        loop(1, groups, lambda h: remote(ref, ref, sg_s, sg_r, other(h)).start())
        if groups > 1:
            total_wait(stat.at[pl.ds(group_stat, groups - 1)], sg_s, sg_r).wait_recv()
        acc = stat[group_stat]
        for h in range(1, groups):
            acc = acc + stat[group_stat + h]
        damping = damp_fraction * 2.0 * jnp.sum(
            jnp.sum(acc, axis=0, keepdims=True), axis=1, keepdims=True
        ) / (tokens * width)
        damp_ref[...] = jnp.broadcast_to(damping, damp_ref.shape)
        diag = scale * acc + damping
        inverse = 1.0 / diag
        for j in range(stat_rows):
            inv[:, j * 128 : (j + 1) * 128] = jnp.broadcast_to(inverse[j : j + 1, :], (8, 128))
        row = lax.broadcasted_iota(jnp.int32, (block, 128), 0)
        lane = lax.broadcasted_iota(jnp.int32, (block, 128), 1)
        every = jnp.sum(jnp.where(row == lane, diag[0:1, :], 0.0), axis=1, keepdims=True)
        row8 = lax.broadcasted_iota(jnp.int32, (8, 128), 0) + core * half + me * 8
        lane8 = lax.broadcasted_iota(jnp.int32, (8, 128), 1)
        unit = jnp.where(row8 == lane8, 1.0, 0.0)
        own_diag = jnp.sum(unit * diag[0:1, :], axis=1, keepdims=True)
        diag_ref[...] = own_diag
        rho_ref[...] = jnp.broadcast_to(1.0 / own_diag, (8, 128))
        rs[...] = jnp.zeros_like(rs)
        ds[...] = jnp.zeros_like(ds)
        xs[...] = jnp.zeros_like(xs)
        rs[:, 0:128] = unit
        ds[:, 0:128] = unit / own_diag
        scaled = cz[...] / every
        cz[...] = scaled
        inner[...] = scaled
        pair_stats().wait_send()
        total_wait(stat.at[pl.ds(member_stat, peers)], sm_s, sm_r).wait_send()
        if groups > 1:
            total_wait(stat.at[pl.ds(group_stat, groups - 1)], sg_s, sg_r).wait_send()

    one = jnp.where(
        lax.broadcasted_iota(jnp.int32, (block, 128), 0) == lax.broadcasted_iota(jnp.int32, (block, 128), 1), 1.0, 0.0
    )
    turned = lax.dot_general(
        one.astype(jnp.bfloat16), c_ref[:, 0:block], (((1,), (1,)), ((), ())), preferred_element_type=f32
    )
    cz[...] = turned
    lhs = turned.astype(jnp.bfloat16)
    product(lhs, 1, 0)
    pl.semaphore_wait(barrier, n)
    pair(0).start()
    for c in range(1, CHUNKS):
        product(lhs, 1, c)
        pair(c).start()
    stat[local_stat] = jnp.zeros(stat.shape[1:], f32)
    for j in range(stat_rows):
        square = c_ref[:, j * 128 : (j + 1) * 128].astype(f32)
        stat[local_stat, j : j + 1, :] = jnp.sum(square * square, axis=0, keepdims=True)
    pair_stats().start()
    wg_ref[label] = w_ref[...]
    mg_ref[columns(label)] = m_ref[...]
    reduce_and_apply(0, True)
    share = -(-(nl - 1) // (steps - 1))

    def iteration(index, carry):
        lhs = two_terms(inner[...])
        for c in range(CHUNKS):
            product(lhs, 2, c)
            pair(c).start()
        finish_sends()
        begin = 1 + (index - 1) * share
        loop(begin, jnp.minimum(begin + share, nl), lambda e: [copy.start() for copy in beside(e, False)])
        reduce_and_apply(lax.rem(index, 2), False)
        return carry

    lax.fori_loop(1, steps, iteration, 0)

    energy = inner[...]
    local_ref[...] = lax.dot_general(
        jnp.ones((8, energy.shape[1]), f32),
        energy * energy,
        (((1,), (1,)), ((), ())),
        precision=lax.Precision.HIGHEST,
        preferred_element_type=f32,
    )
    near = remote(local_ref, part, e_s, e_r, partner)
    near.start()
    near_own = pl.ds(pl.multiple_of(core * half + me * 8, 8), 8)

    def message(at):
        begin = pl.multiple_of(window_start(at, block, cols, window, width), 128)
        view = pl.ds(begin, window)
        return begin, view

    lane8 = lax.broadcasted_iota(jnp.int32, (8, 128), 1)
    power = jnp.sum(ds[...] * ds[...], axis=1, keepdims=True)
    facts = jnp.where(lane8 < 64, rho_ref[...], power)

    def fill(ref, at, place_):
        begin, view = message(at)
        ref[place_ + (slice(0, 128),)] = xs[:, 0:128]
        ref[place_ + (slice(128, 128 + window),)] = xs[:, view]
        ref[place_ + (slice(128 + window, 256 + window),)] = ds[:, 0:128]
        ref[place_ + (slice(256 + window, 256 + 2 * window),)] = ds[:, view]
        ref[place_ + (slice(256 + 2 * window, 384 + 2 * window),)] = facts

    def tell(d):
        e = MEMBERS - 1 - d
        to, g = member(e)
        fill(gs, to[1], (e, slice(None)))
        remote(gs.at[e], gb.at[mine], g_s, g_r, to).start()

    near.wait_recv()
    slots[chip] = local_ref[...] + part[...]

    def far(d, j):
        return remote(slots.at[j], slots.at[j], en_s, en_r, chip_device(d))

    loop(1, n, lambda d: far(d, chip).start())
    loop(0, peers, tell)
    fill(gb, label, (near_own,))
    finish_sends()
    loop(1, nl, lambda e: [copy.wait_recv() for copy in beside(e, True)])
    loop(1, nl, lambda e: [copy.wait_send() for copy in beside(e, False)])
    total_wait(slots.at[pl.ds(0, n - 1)], en_s, en_r).wait_recv()
    norms = lax.fori_loop(1, n, lambda j, acc: acc + slots[j], slots[0])
    total_wait(gb.at[pl.ds(0, peers * 8)], g_s, g_r).wait_recv()
    last = remote(gb.at[half_rows], gb.at[half_rows], gf_s, gf_r, partner)
    last.start()
    near.wait_send()
    total_wait(slots.at[pl.ds(0, n - 1)], en_s, en_r).wait_send()
    total_wait(gs.at[pl.ds(1, peers)], g_s, g_r).wait_send()
    last.wait_recv()
    curve = scale * jnp.sum(one * norms[0:1, :], axis=1, keepdims=True)
    rho = gb[:, 256 + 2 * window : 257 + 2 * window]
    power = gb[:, 320 + 2 * window : 321 + 2 * window]
    alpha = rho / (curve + damp_ref[0:1, 0:1] * power)
    top_ref[...] = gb[:, 0:128] + alpha * gb[:, 128 + window : 256 + window]
    win_ref[...] = gb[:, 128 : 128 + window] + alpha * gb[:, 256 + window : 256 + 2 * window]
    last.wait_send()


def conjugate_gradients(calib, w, mask, block, cols, tokens, nd, nl):
    width = calib.shape[1]
    window = window_width(block, cols, nl)
    nx = math.isqrt(nl // 2)
    groups = (nx // 2) * (nd // 4) * (nl // nx // 2)
    n = nd // 2 * nl
    chunk = width // CHUNKS
    f32, bf16 = jnp.float32, jnp.bfloat16
    vmem = pl.BlockSpec(memory_space=pltpu.VMEM)
    dma = pltpu.SemaphoreType.DMA
    stat_rows = -(-(width // 128) // 8) * 8
    message = 384 + 2 * window
    return pl.pallas_call(
        functools.partial(cg_kernel, nd, nl, cols, tokens),
        out_shape=(
            jax.ShapeDtypeStruct((block, 128), f32),
            jax.ShapeDtypeStruct((block, window), f32),
            jax.ShapeDtypeStruct((nl,) + w.shape, w.dtype),
            jax.ShapeDtypeStruct((mask.shape[0], mask.shape[1] * nl), mask.dtype),
        ),
        in_specs=[vmem] * 3,
        out_specs=(vmem,) * 4,
        scratch_shapes=[
            pltpu.VMEM((CHUNKS, block, chunk), f32),
            pltpu.VMEM((CHUNKS, block // 2, chunk), f32),
            pltpu.VMEM((CHUNKS, MEMBERS, 8, chunk), f32),
            pltpu.VMEM((CHUNKS, MEMBERS, 8, chunk), f32),
            pltpu.VMEM((2, CHUNKS, groups, 8, chunk), f32),
            pltpu.VMEM((CHUNKS, 2 * block, chunk), bf16),
            pltpu.VMEM((block, 128), f32),
            pltpu.VMEM((8, width), f32),
            pltpu.VMEM((8, width), f32),
            pltpu.VMEM((8, width), f32),
            pltpu.VMEM((8, width), f32),
            pltpu.VMEM((8, width), f32),
            pltpu.VMEM((8, 128), f32),
            pltpu.VMEM((8, 1), f32),
            pltpu.VMEM((8, 128), f32),
            pltpu.VMEM((block, calib.shape[0]), f32),
            pltpu.VMEM((block, calib.shape[0]), f32),
            pltpu.VMEM((2 + MEMBERS + groups, stat_rows, 128), f32),
            pltpu.VMEM((MEMBERS, 8, message), f32),
            pltpu.VMEM((block, message), f32),
            pltpu.VMEM((8, block), f32),
            pltpu.VMEM((8, block), f32),
            pltpu.VMEM((n, 8, block), f32),
        ]
        + [dma((CHUNKS,))] * 4
        + [dma((2, CHUNKS))] * 2
        + [dma((CHUNKS,))] * 4
        + [dma] * 4
        + [dma] * 6
        + [dma] * 4
        + [dma] * 4
        + [dma((nl,))] * 4,
        compiler_params=pltpu.CompilerParams(collective_id=0, has_side_effects=True, vmem_limit_bytes=48 << 20),
        name="conjugate_gradients",
    )(calib, w, mask)


def prune_kernel(w_ref, m_ref, l_ref, t_ref, kept_ref, err_ref, cross_ref):
    block = w_ref.shape[0]
    err_ref[...] = jnp.zeros_like(err_ref)
    cross_ref[...] = jnp.zeros_like(cross_ref)

    def earlier(factor, ref):
        return jnp.dot(factor, ref[...], precision=lax.Precision.HIGHEST, preferred_element_type=jnp.float32)

    for begin in range(0, block, sub_width):
        rows = pl.ds(begin, sub_width)
        window = w_ref[rows, :].astype(jnp.float32)
        target = t_ref[rows, :]
        chosen = m_ref[rows, :].astype(jnp.float32)
        factor = l_ref[rows, :]
        if begin:
            window = window - earlier(factor, err_ref)
            target = target - earlier(factor, cross_ref)
        for offset in range(sub_width):
            index = begin + offset
            one = slice(offset, offset + 1)
            column = factor[:, index : index + 1]
            inverse = 1.0 / factor[one, index : index + 1]
            error = chosen[one, :] * window[one, :] * inverse
            solved = target[one, :] * inverse
            err_ref[index : index + 1, :] = error
            cross_ref[index : index + 1, :] = solved
            window = window - column * error
            target = target - column * solved
        kept_ref[rows, :] = ((1.0 - chosen) * window).astype(kept_ref.dtype)


def prune_rows(weights, mask, lower, target):
    block, rows = weights.shape
    tile = min(rows, 2048)
    spec = pl.BlockSpec((block, tile), lambda i: (0, i))
    fixed = [pl.BlockSpec(x.shape, lambda i: (0, 0)) for x in (lower, target)]
    return pl.pallas_call(
        prune_kernel,
        grid=(rows // tile,),
        out_shape=(
            jax.ShapeDtypeStruct((block, rows), jnp.bfloat16),
            jax.ShapeDtypeStruct((block, rows), jnp.float32),
            jax.ShapeDtypeStruct(target.shape, jnp.float32),
        ),
        in_specs=[spec, spec] + fixed,
        out_specs=(spec, spec, fixed[1]),
        compiler_params=pltpu.CompilerParams(vmem_limit_bytes=32 << 20),
        name="prune_rows",
    )(weights, mask, lower, target)


def per_device(calib, block_weight, rest_weight, prune_mask):
    block = prune_mask.shape[1]
    nd, nl = lax.axis_size("dp"), lax.axis_size("label")
    own = prune_mask.shape[0]
    label = lax.axis_index("label")
    width = calib.shape[1]
    rest_cols = rest_weight.shape[1]
    top, near, weights, mask = conjugate_gradients(
        calib,
        block_weight.T,
        prune_mask.T.astype(jnp.bfloat16),
        block,
        rest_cols,
        calib.shape[0] * nd * nl,
        nd,
        nl,
    )
    weights = weights.reshape(block, -1)
    top = 0.5 * (top + top.T)
    lower = jnp.linalg.cholesky(top)
    begin = window_start(label, block, rest_cols, near.shape[1], width)
    owned = lax.dynamic_slice_in_dim(near, block + label * rest_cols - begin, rest_cols, 1)
    kept, errors, cross = prune_rows(weights, mask, lower, owned)
    pruned_block = lax.dynamic_slice_in_dim(kept, label * own, own, 1).T
    delta = lax.dot_general(
        errors,
        cross,
        (((0,), (0,)), ((), ())),
        precision=lax.Precision.HIGHEST,
        preferred_element_type=jnp.float32,
    )
    updated_rest = (rest_weight.astype(jnp.float32) - delta).astype(jnp.bfloat16)
    return (pruned_block, updated_rest)


def solution(mesh):
    return jax.shard_map(
        per_device,
        mesh=mesh,
        in_specs=(
            P(("dp", "label"), None),
            P("dp", "label"),
            P("dp", "label"),
            P(("dp", "label"), None),
        ),
        out_specs=(P(("dp", "label"), None), P("dp", "label")),
        check_vma=False,
    )
```

```python
import functools
import math

import jax
import jax.numpy as jnp
from jax import lax
from jax.experimental import pallas as pl
from jax.experimental.pallas import tpu as pltpu
from jax.sharding import PartitionSpec as P

ITERS = 6
MESH = pl.DeviceIdType.MESH

damp_fraction = 0.01
sub_width = 16
CHUNKS = 3
MEMBERS = 8


def two_terms(x):
    high = x.astype(jnp.bfloat16)
    low = (x - high.astype(jnp.float32)).astype(jnp.bfloat16)
    return jnp.concatenate([high, low], axis=0)


def loop(low, high, body):
    def step(d, carry):
        body(d)
        return carry

    lax.fori_loop(low, high, step, 0)


def remote(src, dst, send, recv, to):
    return pltpu.make_async_remote_copy(
        src_ref=src, dst_ref=dst, send_sem=send, recv_sem=recv, device_id=to, device_id_type=MESH
    )


def window_start(label, block, cols, window, width):
    return jnp.minimum((block + label * cols) // 128, (width - window) // 128) * 128


def window_width(block, cols, nl):
    return max(-(-((block + at * cols) % 128 + cols) // 128) * 128 for at in range(nl))


def place(nd, nl):
    nx = math.isqrt(nl // 2)
    ny, nz = nd // 2, nl // nx
    groups = (nx // 2) * (ny // 2) * (nz // 2)
    dp = lax.axis_index("dp")
    label = lax.axis_index("label")
    core, y, z, x = lax.rem(dp, 2), dp // 2, label // nx, lax.rem(label, nx)
    mx, my, mz = lax.rem(x, 2), lax.rem(y, 2), lax.rem(z, 2)
    qx, qy, qz = x // 2, y // 2, z // 2
    group = (qz * (ny // 2) + qy) * (nx // 2) + qx

    def member(e):
        hx, hy, hz = lax.rem(mx + lax.rem(e, 2), 2), lax.rem(my + lax.rem(e // 2, 2), 2), lax.rem(mz + e // 4, 2)
        return ((qy * 2 + hy) * 2 + core, (qz * 2 + hz) * nx + qx * 2 + hx), hz * 4 + hy * 2 + hx

    def other(h):
        q = lax.rem(group + h, groups)
        hx, hy, hz = lax.rem(q, nx // 2), lax.rem(q // (nx // 2), ny // 2), q // ((nx // 2) * (ny // 2))
        return ((hy * 2 + my) * 2 + core, (hz * 2 + mz) * nx + hx * 2 + mx)

    partner = (dp + 1 - 2 * core, label)
    return core, mz * 4 + my * 2 + mx, group, groups, member, other, partner


def cg_kernel(
    nd, nl, cols, tokens, c_ref, w_ref, m_ref, top_ref, win_ref, wg_ref, mg_ref,
    x_ref, pbuf, sbuf, rbuf, stbuf, vb, ab, img, xs, rs, ds, inv, damp_ref, diag_ref, rho_ref,
    cz, inner, stat, gs, gb, local_ref, part, slots,
    pair_s, pair_r, rs_s, rs_r, st_s, st_r, ag_s, ag_r, fw_s, fw_r, ab_s, ab_r, abf_s, abf_r,
    sp_s, sp_r, sm_s, sm_r, sg_s, sg_r, g_s, g_r, gf_s, gf_r, e_s, e_r, en_s, en_r, wsend, wrecv, msend, mrecv,
):
    block = top_ref.shape[0]
    width = c_ref.shape[1]
    window = win_ref.shape[1]
    chunk = width // CHUNKS
    half = block // 2
    peers = MEMBERS - 1
    stat_rows = width // 128
    steps = ITERS - 1
    f32 = jnp.float32
    scale = 2.0 / tokens
    core, me, group, groups, member, other, partner = place(nd, nl)
    dp = lax.axis_index("dp")
    label = lax.axis_index("label")
    n = (nd // 2) * nl
    chip = (dp // 2) * nl + label
    own = m_ref.shape[1]

    def lanes(c):
        return pl.ds(c * chunk, chunk)

    def rows8(core_, g):
        return pl.ds(pl.multiple_of(core_ * half + g * 8, 8), 8)

    def rows16(core_, g):
        return pl.ds(pl.multiple_of(core_ * 2 * half + g * 16, 16), 16)

    half_rows = pl.ds(pl.multiple_of(core * half, half), half)
    away_rows = pl.ds(pl.multiple_of((1 - core) * half, half), half)
    half_rows16 = pl.ds(pl.multiple_of(core * 2 * half, 2 * half), 2 * half)
    mine = rows8(core, me)

    def chip_device(d):
        j = lax.rem(chip + d, n)
        return (2 * (j // nl) + core, lax.rem(j, nl))

    def columns(at):
        return (slice(None), pl.ds(pl.multiple_of(at * own, 128), own))

    def beside(e, arriving):
        to = lax.rem(label + (nl - e if arriving else e), nl)
        at = to if arriving else label
        return (
            remote(w_ref, wg_ref.at[at], wsend.at[e], wrecv.at[e], (dp, to)),
            remote(m_ref, mg_ref.at[columns(at)], msend.at[e], mrecv.at[e], (dp, to)),
        )

    def pair(c):
        return remote(x_ref.at[c, away_rows], pbuf.at[c], pair_s.at[c], pair_r.at[c], partner)

    def forward(c):
        ref = vb.at[c, half_rows16]
        return remote(ref, ref, fw_s.at[c], fw_r.at[c], partner)

    def forward_ab():
        ref = ab.at[half_rows]
        return remote(ref, ref, abf_s, abf_r, partner)

    def total_wait(ref, send, recv):
        return remote(ref, ref, send, recv, partner)

    barrier = pltpu.get_barrier_semaphore()
    pl.semaphore_signal(barrier, inc=1, device_id=partner, device_id_type=MESH)
    loop(1, n, lambda d: pl.semaphore_signal(barrier, inc=1, device_id=chip_device(d), device_id_type=MESH))

    def product(lhs, terms, c):
        out = jnp.dot(lhs, c_ref[:, lanes(c)], preferred_element_type=f32)
        x_ref[c] = out[:block] + out[block:] if terms == 2 else out

    def scatter(c):
        pair(c).wait_recv()

        def send(d):
            e = MEMBERS - 1 - d
            to, g = member(e)
            sbuf[c, e] = x_ref[c, rows8(core, g)] + pbuf[c, pl.ds(pl.multiple_of(g * 8, 8), 8)]
            remote(sbuf.at[c, e], rbuf.at[c, e], rs_s.at[c], rs_r.at[c], to).start()

        loop(0, peers, send)

    def cross(c, par):
        acc = x_ref[c, mine] + pbuf[c, pl.ds(pl.multiple_of(me * 8, 8), 8)]
        total_wait(rbuf.at[c, pl.ds(1, peers)], rs_s.at[c], rs_r.at[c]).wait_recv()
        for e in range(1, MEMBERS):
            acc = acc + rbuf[c, e]
        stbuf[par, c, group] = acc
        ref = stbuf.at[par, c, group]
        loop(1, groups, lambda h: remote(ref, ref, st_s.at[par, c], st_r.at[par, c], other(h)).start())

    def crossed(c, par, first):
        if groups > 1:
            total_wait(stbuf.at[par, c, pl.ds(0, groups - 1)], st_s.at[par, c], st_r.at[par, c]).wait_recv()
        acc = stbuf[par, c, 0]
        for h in range(1, groups):
            acc = acc + stbuf[par, c, h]
        if first:
            acc = acc / diag_ref[...]
        direction = ds[:, lanes(c)]
        image = scale * acc + damp_ref[0:8, 0:1] * direction
        img[:, lanes(c)] = image
        vb[c, rows16(core, me)] = two_terms(image * inv[:, lanes(c)])

        def send(d):
            to, g = member(MEMBERS - 1 - d)
            ref = vb.at[c, rows16(core, me)]
            remote(ref, ref, ag_s.at[c], ag_r.at[c], to).start()

        loop(0, peers, send)
        return jnp.sum(direction * image, axis=1, keepdims=True)

    def rescale(curve):
        rho = rho_ref[:, 0:1]
        alpha = rho / curve
        fresh = jnp.zeros((8, 1), f32)
        for c in range(CHUNKS):
            resid = rs[:, lanes(c)] - alpha * img[:, lanes(c)]
            rs[:, lanes(c)] = resid
            fresh = fresh + jnp.sum(resid * resid * inv[:, lanes(c)], axis=1, keepdims=True)
        beta = fresh / rho
        lane = lax.broadcasted_iota(jnp.int32, (8, 128), 1)
        ab[mine] = jnp.where(lane < 64, alpha, beta)

        def send(d):
            to, g = member(MEMBERS - 1 - d)
            remote(ab.at[mine], ab.at[mine], ab_s, ab_r, to).start()

        loop(0, peers, send)
        rho_ref[...] = jnp.broadcast_to(fresh, (8, 128))
        for c in range(CHUNKS):
            direction = ds[:, lanes(c)]
            xs[:, lanes(c)] = xs[:, lanes(c)] + alpha * direction
            ds[:, lanes(c)] = rs[:, lanes(c)] * inv[:, lanes(c)] + beta * direction

    def gather(c):
        total_wait(vb.at[c, pl.ds(0, peers * 16)], ag_s.at[c], ag_r.at[c]).wait_recv()
        forward(c).start()

    def applied(c):
        forward(c).wait_recv()
        return lax.dot_general(
            vb[c], c_ref[:, lanes(c)], (((1,), (1,)), ((), ())), preferred_element_type=f32
        )

    def finish_sends():
        for c in range(CHUNKS):
            total_wait(vb.at[c, pl.ds(0, peers * 16)], ag_s.at[c], ag_r.at[c]).wait_send()
            forward(c).wait_send()
        total_wait(ab.at[pl.ds(0, peers * 8)], ab_s, ab_r).wait_send()
        forward_ab().wait_send()

    def reduce_and_apply(par, first):
        for c in range(CHUNKS):
            scatter(c)
        if first:
            share_stats()
        for c in range(CHUNKS):
            cross(c, par)
        for c in range(CHUNKS):
            pair(c).wait_send()
            total_wait(sbuf.at[c, pl.ds(1, peers)], rs_s.at[c], rs_r.at[c]).wait_send()
        if first:
            start_state()
        curve = jnp.zeros((8, 1), f32)
        for c in range(CHUNKS):
            curve = curve + crossed(c, par, first)
        rescale(curve)
        for c in range(CHUNKS):
            gather(c)
        total_wait(ab.at[pl.ds(0, peers * 8)], ab_s, ab_r).wait_recv()
        forward_ab().start()
        if groups > 1:
            for c in range(CHUNKS):
                total_wait(stbuf.at[par, c, pl.ds(0, groups - 1)], st_s.at[par, c], st_r.at[par, c]).wait_send()
        out = applied(0)
        for c in range(1, CHUNKS):
            out = out + applied(c)
        forward_ab().wait_recv()
        out = out.reshape(2 * block // 16, 2, 8, out.shape[1])
        out = (out[:, 0] + out[:, 1]).reshape(block, out.shape[3])
        applied_z = cz[...] - ab[:, 0:1] * out
        cz[...] = applied_z
        inner[...] = applied_z + ab[:, 64:65] * inner[...]

    local_stat, near_stat, member_stat, group_stat = 0, 1, 2, 2 + MEMBERS

    def pair_stats():
        return remote(stat.at[local_stat], stat.at[near_stat], sp_s, sp_r, partner)

    def share_stats():
        pair_stats().wait_recv()
        stat[member_stat + me] = stat[local_stat] + stat[near_stat]
        ref = stat.at[member_stat + me]
        loop(1, MEMBERS, lambda e: remote(ref, ref, sm_s, sm_r, member(e)[0]).start())

    def start_state():
        total_wait(stat.at[pl.ds(member_stat, peers)], sm_s, sm_r).wait_recv()
        acc = stat[member_stat]
        for e in range(1, MEMBERS):
            acc = acc + stat[member_stat + e]
        stat[group_stat + group] = acc
        ref = stat.at[group_stat + group]
        loop(1, groups, lambda h: remote(ref, ref, sg_s, sg_r, other(h)).start())
        if groups > 1:
            total_wait(stat.at[pl.ds(group_stat, groups - 1)], sg_s, sg_r).wait_recv()
        acc = stat[group_stat]
        for h in range(1, groups):
            acc = acc + stat[group_stat + h]
        damping = damp_fraction * 2.0 * jnp.sum(
            jnp.sum(acc, axis=0, keepdims=True), axis=1, keepdims=True
        ) / (tokens * width)
        damp_ref[...] = jnp.broadcast_to(damping, damp_ref.shape)
        diag = scale * acc + damping
        inverse = 1.0 / diag
        for j in range(stat_rows):
            inv[:, j * 128 : (j + 1) * 128] = jnp.broadcast_to(inverse[j : j + 1, :], (8, 128))
        row = lax.broadcasted_iota(jnp.int32, (block, 128), 0)
        lane = lax.broadcasted_iota(jnp.int32, (block, 128), 1)
        every = jnp.sum(jnp.where(row == lane, diag[0:1, :], 0.0), axis=1, keepdims=True)
        row8 = lax.broadcasted_iota(jnp.int32, (8, 128), 0) + core * half + me * 8
        lane8 = lax.broadcasted_iota(jnp.int32, (8, 128), 1)
        unit = jnp.where(row8 == lane8, 1.0, 0.0)
        own_diag = jnp.sum(unit * diag[0:1, :], axis=1, keepdims=True)
        diag_ref[...] = own_diag
        rho_ref[...] = jnp.broadcast_to(1.0 / own_diag, (8, 128))
        rs[...] = jnp.zeros_like(rs)
        ds[...] = jnp.zeros_like(ds)
        xs[...] = jnp.zeros_like(xs)
        rs[:, 0:128] = unit
        ds[:, 0:128] = unit / own_diag
        scaled = cz[...] / every
        cz[...] = scaled
        inner[...] = scaled
        pair_stats().wait_send()
        total_wait(stat.at[pl.ds(member_stat, peers)], sm_s, sm_r).wait_send()
        if groups > 1:
            total_wait(stat.at[pl.ds(group_stat, groups - 1)], sg_s, sg_r).wait_send()

    one = jnp.where(
        lax.broadcasted_iota(jnp.int32, (block, 128), 0) == lax.broadcasted_iota(jnp.int32, (block, 128), 1), 1.0, 0.0
    )
    turned = lax.dot_general(
        one.astype(jnp.bfloat16), c_ref[:, 0:block], (((1,), (1,)), ((), ())), preferred_element_type=f32
    )
    cz[...] = turned
    lhs = turned.astype(jnp.bfloat16)
    product(lhs, 1, 0)
    pl.semaphore_wait(barrier, n)
    pair(0).start()
    for c in range(1, CHUNKS):
        product(lhs, 1, c)
        pair(c).start()
    stat[local_stat] = jnp.zeros(stat.shape[1:], f32)
    for j in range(stat_rows):
        square = c_ref[:, j * 128 : (j + 1) * 128].astype(f32)
        stat[local_stat, j : j + 1, :] = jnp.sum(square * square, axis=0, keepdims=True)
    pair_stats().start()
    wg_ref[label] = w_ref[...]
    mg_ref[columns(label)] = m_ref[...]
    reduce_and_apply(0, True)
    share = -(-(nl - 1) // (steps - 1))

    def iteration(index, carry):
        lhs = two_terms(inner[...])
        for c in range(CHUNKS):
            product(lhs, 2, c)
            pair(c).start()
        finish_sends()
        begin = 1 + (index - 1) * share
        loop(begin, jnp.minimum(begin + share, nl), lambda e: [copy.start() for copy in beside(e, False)])
        reduce_and_apply(lax.rem(index, 2), False)
        return carry

    lax.fori_loop(1, steps, iteration, 0)

    energy = inner[...]
    local_ref[...] = lax.dot_general(
        jnp.ones((8, energy.shape[1]), f32),
        energy * energy,
        (((1,), (1,)), ((), ())),
        precision=lax.Precision.HIGHEST,
        preferred_element_type=f32,
    )
    near = remote(local_ref, part, e_s, e_r, partner)
    near.start()
    near_own = pl.ds(pl.multiple_of(core * half + me * 8, 8), 8)

    def message(at):
        begin = pl.multiple_of(window_start(at, block, cols, window, width), 128)
        view = pl.ds(begin, window)
        return begin, view

    lane8 = lax.broadcasted_iota(jnp.int32, (8, 128), 1)
    power = jnp.sum(ds[...] * ds[...], axis=1, keepdims=True)
    facts = jnp.where(lane8 < 64, rho_ref[...], power)

    def fill(ref, at, place_):
        begin, view = message(at)
        ref[place_ + (slice(0, 128),)] = xs[:, 0:128]
        ref[place_ + (slice(128, 128 + window),)] = xs[:, view]
        ref[place_ + (slice(128 + window, 256 + window),)] = ds[:, 0:128]
        ref[place_ + (slice(256 + window, 256 + 2 * window),)] = ds[:, view]
        ref[place_ + (slice(256 + 2 * window, 384 + 2 * window),)] = facts

    def tell(d):
        e = MEMBERS - 1 - d
        to, g = member(e)
        fill(gs, to[1], (e, slice(None)))
        remote(gs.at[e], gb.at[mine], g_s, g_r, to).start()

    near.wait_recv()
    slots[chip] = local_ref[...] + part[...]

    def far(d, j):
        return remote(slots.at[j], slots.at[j], en_s, en_r, chip_device(d))

    loop(1, n, lambda d: far(d, chip).start())
    loop(0, peers, tell)
    fill(gb, label, (near_own,))
    finish_sends()
    loop(1, nl, lambda e: [copy.wait_recv() for copy in beside(e, True)])
    loop(1, nl, lambda e: [copy.wait_send() for copy in beside(e, False)])
    total_wait(slots.at[pl.ds(0, n - 1)], en_s, en_r).wait_recv()
    norms = lax.fori_loop(1, n, lambda j, acc: acc + slots[j], slots[0])
    total_wait(gb.at[pl.ds(0, peers * 8)], g_s, g_r).wait_recv()
    last = remote(gb.at[half_rows], gb.at[half_rows], gf_s, gf_r, partner)
    last.start()
    near.wait_send()
    total_wait(slots.at[pl.ds(0, n - 1)], en_s, en_r).wait_send()
    total_wait(gs.at[pl.ds(1, peers)], g_s, g_r).wait_send()
    last.wait_recv()
    curve = scale * jnp.sum(one * norms[0:1, :], axis=1, keepdims=True)
    rho = gb[:, 256 + 2 * window : 257 + 2 * window]
    power = gb[:, 320 + 2 * window : 321 + 2 * window]
    alpha = rho / (curve + damp_ref[0:1, 0:1] * power)
    top_ref[...] = gb[:, 0:128] + alpha * gb[:, 128 + window : 256 + window]
    win_ref[...] = gb[:, 128 : 128 + window] + alpha * gb[:, 256 + window : 256 + 2 * window]
    last.wait_send()


def conjugate_gradients(calib, w, mask, block, cols, tokens, nd, nl):
    width = calib.shape[1]
    window = window_width(block, cols, nl)
    nx = math.isqrt(nl // 2)
    groups = (nx // 2) * (nd // 4) * (nl // nx // 2)
    n = nd // 2 * nl
    chunk = width // CHUNKS
    f32, bf16 = jnp.float32, jnp.bfloat16
    vmem = pl.BlockSpec(memory_space=pltpu.VMEM)
    dma = pltpu.SemaphoreType.DMA
    stat_rows = -(-(width // 128) // 8) * 8
    message = 384 + 2 * window
    return pl.pallas_call(
        functools.partial(cg_kernel, nd, nl, cols, tokens),
        out_shape=(
            jax.ShapeDtypeStruct((block, 128), f32),
            jax.ShapeDtypeStruct((block, window), f32),
            jax.ShapeDtypeStruct((nl,) + w.shape, w.dtype),
            jax.ShapeDtypeStruct((mask.shape[0], mask.shape[1] * nl), mask.dtype),
        ),
        in_specs=[vmem] * 3,
        out_specs=(vmem,) * 4,
        scratch_shapes=[
            pltpu.VMEM((CHUNKS, block, chunk), f32),
            pltpu.VMEM((CHUNKS, block // 2, chunk), f32),
            pltpu.VMEM((CHUNKS, MEMBERS, 8, chunk), f32),
            pltpu.VMEM((CHUNKS, MEMBERS, 8, chunk), f32),
            pltpu.VMEM((2, CHUNKS, groups, 8, chunk), f32),
            pltpu.VMEM((CHUNKS, 2 * block, chunk), bf16),
            pltpu.VMEM((block, 128), f32),
            pltpu.VMEM((8, width), f32),
            pltpu.VMEM((8, width), f32),
            pltpu.VMEM((8, width), f32),
            pltpu.VMEM((8, width), f32),
            pltpu.VMEM((8, width), f32),
            pltpu.VMEM((8, 128), f32),
            pltpu.VMEM((8, 1), f32),
            pltpu.VMEM((8, 128), f32),
            pltpu.VMEM((block, calib.shape[0]), f32),
            pltpu.VMEM((block, calib.shape[0]), f32),
            pltpu.VMEM((2 + MEMBERS + groups, stat_rows, 128), f32),
            pltpu.VMEM((MEMBERS, 8, message), f32),
            pltpu.VMEM((block, message), f32),
            pltpu.VMEM((8, block), f32),
            pltpu.VMEM((8, block), f32),
            pltpu.VMEM((n, 8, block), f32),
        ]
        + [dma((CHUNKS,))] * 4
        + [dma((2, CHUNKS))] * 2
        + [dma((CHUNKS,))] * 4
        + [dma] * 4
        + [dma] * 6
        + [dma] * 4
        + [dma] * 4
        + [dma((nl,))] * 4,
        compiler_params=pltpu.CompilerParams(collective_id=0, has_side_effects=True, vmem_limit_bytes=48 << 20),
        name="conjugate_gradients",
    )(calib, w, mask)


def finish_kernel(w_ref, m_ref, top_ref, t_ref, rest_ref, kept_ref, out_ref, sym, lower, tri, scales, errors, kept):
    block, rows = w_ref.shape
    own = kept_ref.shape[0]
    cols = rest_ref.shape[0]
    width = tri.shape[1]
    f32, bf16 = jnp.float32, jnp.bfloat16
    group = 512 if rows % 512 == 0 else rows
    top = top_ref[...]
    sym[...] = 0.5 * (top + top.T)
    lower[...] = jnp.zeros_like(lower)
    errors[...] = jnp.zeros_like(errors)
    tri[...] = jnp.zeros_like(tri)
    row = lax.broadcasted_iota(jnp.int32, (sub_width, 128), 0)

    def wide(x, lanes):
        return jnp.concatenate([x] * (lanes // 128), axis=1)

    def split(x):
        high = x.astype(bf16)
        return high, (x - high.astype(f32)).astype(bf16)

    for begin in range(0, block, sub_width):
        at = slice(begin, begin + sub_width)
        target = jnp.concatenate([sym[at, :], t_ref[at, :]], axis=1)
        if begin:
            factor = lower[...].T[at, :]
            target = target - jnp.dot(
                factor, tri[...], precision=lax.Precision.HIGHEST, preferred_element_type=f32
            )
            high, low = split(factor)
            factors = jnp.concatenate(
                [jnp.concatenate([high, high], axis=1), jnp.concatenate([low, jnp.zeros_like(low)], axis=1)], axis=0
            )
        spread = [
            jnp.broadcast_to(target[:, begin + j : begin + j + 1], (sub_width, 128)) for j in range(sub_width)
        ]
        steps = []
        inverses = []
        for j in range(sub_width):
            inverse = 1.0 / spread[j][j : j + 1, :]
            step = jnp.where(row > j, spread[j] * inverse, 0.0)
            for k in range(j + 1, sub_width):
                spread[k] = spread[k] - step * spread[k][j : j + 1, :]
            steps.append(step)
            inverses.append(inverse)
        for j in range(sub_width):
            target = target - wide(steps[j], width) * target[j : j + 1, :]
        tri[at, :] = target
        inverse = jnp.concatenate(inverses, axis=0)
        scales[at, :] = inverse
        lower[at, :] = target[:, :block] * inverse
        for first in range(0, rows, group):
            lanes = slice(first, first + group)
            window = w_ref[at, lanes].astype(f32)
            chosen = m_ref[at, lanes].astype(f32)
            if begin:
                both = jnp.dot(factors, errors[:, lanes], preferred_element_type=f32)
                window = window - (both[:sub_width] + both[sub_width:])
            for j in range(sub_width):
                window = window - wide(steps[j], group) * (chosen[j : j + 1, :] * window[j : j + 1, :])
            error = chosen * window
            high, low = split(error)
            errors[at, lanes] = high
            errors[slice(block + begin, block + begin + sub_width), lanes] = low
            kept[at, lanes] = window - error
    label = lax.axis_index("label")
    kept_ref[...] = kept[:, pl.ds(pl.multiple_of(label * own, 128), own)].T.astype(kept_ref.dtype)
    cross = (tri[:, 128:] * wide(scales[...], width - 128)).T[:cols]
    high, low = split(cross)
    twice = jnp.concatenate([high, high], axis=1)
    for first in range(0, rows, group):
        lanes = slice(first, first + group)
        delta = jnp.dot(twice, errors[:, lanes], preferred_element_type=f32)
        delta = delta + jnp.dot(low, errors[:block, lanes], preferred_element_type=f32)
        out_ref[:, lanes] = (rest_ref[:, lanes].astype(f32) - delta).astype(out_ref.dtype)


def finish(weights, mask, top, target, rest, own):
    block, rows = weights.shape
    cols = rest.shape[0]
    f32, bf16 = jnp.float32, jnp.bfloat16
    padded = -(-cols // 128) * 128
    target = jnp.pad(target, ((0, 0), (0, padded - cols)))
    vmem = pl.BlockSpec(memory_space=pltpu.VMEM)
    return pl.pallas_call(
        finish_kernel,
        out_shape=(jax.ShapeDtypeStruct((own, block), bf16), jax.ShapeDtypeStruct((cols, rows), bf16)),
        in_specs=[vmem] * 5,
        out_specs=(vmem, vmem),
        scratch_shapes=[
            pltpu.VMEM((block, block), f32),
            pltpu.VMEM((block, block), f32),
            pltpu.VMEM((block, 128 + padded), f32),
            pltpu.VMEM((block, 128), f32),
            pltpu.VMEM((2 * block, rows), bf16),
            pltpu.VMEM((block, rows), f32),
        ],
        compiler_params=pltpu.CompilerParams(vmem_limit_bytes=48 << 20),
        name="finish",
    )(weights, mask, top, target, rest)


def per_device(calib, block_weight, rest_weight, prune_mask):
    block = prune_mask.shape[1]
    nd, nl = lax.axis_size("dp"), lax.axis_size("label")
    own = prune_mask.shape[0]
    label = lax.axis_index("label")
    width = calib.shape[1]
    rest_cols = rest_weight.shape[1]
    top, near, weights, mask = conjugate_gradients(
        calib,
        block_weight.T,
        prune_mask.T.astype(jnp.bfloat16),
        block,
        rest_cols,
        calib.shape[0] * nd * nl,
        nd,
        nl,
    )
    weights = weights.reshape(block, -1)
    begin = window_start(label, block, rest_cols, near.shape[1], width)
    owned = lax.dynamic_slice_in_dim(near, block + label * rest_cols - begin, rest_cols, 1)
    pruned_block, updated_rest = finish(weights, mask, top, owned, rest_weight.T, own)
    return (pruned_block, updated_rest.T)


def solution(mesh):
    return jax.shard_map(
        per_device,
        mesh=mesh,
        in_specs=(
            P(("dp", "label"), None),
            P("dp", "label"),
            P("dp", "label"),
            P(("dp", "label"), None),
        ),
        out_specs=(P(("dp", "label"), None), P("dp", "label")),
        check_vma=False,
    )
```

```python
import functools
import math

import jax
import jax.numpy as jnp
from jax import lax
from jax.experimental import pallas as pl
from jax.experimental.pallas import tpu as pltpu
from jax.sharding import PartitionSpec as P

ITERS = 6
MESH = pl.DeviceIdType.MESH

damp_fraction = 0.01
sub_width = 16
CHUNKS = 7
MEMBERS = 8


def two_terms(x):
    high = x.astype(jnp.bfloat16)
    low = (x - high.astype(jnp.float32)).astype(jnp.bfloat16)
    return jnp.concatenate([high, low], axis=0)


def loop(low, high, body):
    def step(d, carry):
        body(d)
        return carry

    lax.fori_loop(low, high, step, 0)


def remote(src, dst, send, recv, to):
    return pltpu.make_async_remote_copy(
        src_ref=src, dst_ref=dst, send_sem=send, recv_sem=recv, device_id=to, device_id_type=MESH
    )


def window_start(label, block, cols, window, width):
    return jnp.minimum((block + label * cols) // 128, (width - window) // 128) * 128


def window_width(block, cols, nl):
    return max(-(-((block + at * cols) % 128 + cols) // 128) * 128 for at in range(nl))


def place(nd, nl):
    nx = math.isqrt(nl // 2)
    ny, nz = nd // 2, nl // nx
    groups = (nx // 2) * (ny // 2) * (nz // 2)
    dp = lax.axis_index("dp")
    label = lax.axis_index("label")
    core, y, z, x = lax.rem(dp, 2), dp // 2, label // nx, lax.rem(label, nx)
    mx, my, mz = lax.rem(x, 2), lax.rem(y, 2), lax.rem(z, 2)
    qx, qy, qz = x // 2, y // 2, z // 2
    group = (qz * (ny // 2) + qy) * (nx // 2) + qx

    def member(e):
        hx, hy, hz = lax.rem(mx + lax.rem(e, 2), 2), lax.rem(my + lax.rem(e // 2, 2), 2), lax.rem(mz + e // 4, 2)
        return ((qy * 2 + hy) * 2 + core, (qz * 2 + hz) * nx + qx * 2 + hx), hz * 4 + hy * 2 + hx

    def other(h):
        q = lax.rem(group + h, groups)
        hx, hy, hz = lax.rem(q, nx // 2), lax.rem(q // (nx // 2), ny // 2), q // ((nx // 2) * (ny // 2))
        return ((hy * 2 + my) * 2 + core, (hz * 2 + mz) * nx + hx * 2 + mx)

    sets = (nx // 2) * (nz // 2)
    here = qz * (nx // 2) + qx

    def twin(h):
        q = lax.rem(here + h, sets)
        return (q // (nx // 2) * 2 + mz) * nx + lax.rem(q, nx // 2) * 2 + mx

    def fellow(j):
        return (qz * 2 + lax.rem(mz + j // 2, 2)) * nx + qx * 2 + lax.rem(mx + lax.rem(j, 2), 2)

    partner = (dp + 1 - 2 * core, label)
    return core, mz * 4 + my * 2 + mx, group, groups, member, other, partner, sets, twin, fellow


def cg_kernel(
    nd, nl, cols, tokens, calib_ref, w_ref, m_ref, top_ref, win_ref, wg_ref, mg_ref,
    c_ref, mask_ref, x_ref, pbuf, sbuf, rbuf, stbuf, vb, ab, img, xs, rs, ds, inv, damp_ref, diag_ref, rho_ref,
    cz, inner, stat, gs, gb, local_ref, part, slots,
    pair_s, pair_r, rs_s, rs_r, st_s, st_r, ag_s, ag_r, fw_s, fw_r, ab_s, ab_r, abf_s, abf_r,
    sp_s, sp_r, sm_s, sm_r, sg_s, sg_r, g_s, g_r, gf_s, gf_r, e_s, e_r, en_s, en_r, wt_s, wt_r, mt_s, mt_r, wf_s, wf_r, mf_s, mf_r, load,
):
    block = top_ref.shape[0]
    width = c_ref.shape[1]
    window = win_ref.shape[1]
    chunk = width // CHUNKS
    half = block // 2
    peers = MEMBERS - 1
    stat_rows = width // 128
    steps = ITERS - 1
    f32 = jnp.float32
    scale = 2.0 / tokens
    core, me, group, groups, member, other, partner, sets, twin, fellow = place(nd, nl)
    dp = lax.axis_index("dp")
    label = lax.axis_index("label")
    n = (nd // 2) * nl
    chip = (dp // 2) * nl + label
    own = m_ref.shape[0]

    def lanes(c):
        return pl.ds(c * chunk, chunk)

    def rows8(core_, g):
        return pl.ds(pl.multiple_of(core_ * half + g * 8, 8), 8)

    def rows16(core_, g):
        return pl.ds(pl.multiple_of(core_ * 2 * half + g * 16, 16), 16)

    half_rows = pl.ds(pl.multiple_of(core * half, half), half)
    away_rows = pl.ds(pl.multiple_of((1 - core) * half, half), half)
    half_rows16 = pl.ds(pl.multiple_of(core * 2 * half, 2 * half), 2 * half)
    mine = rows8(core, me)

    def chip_device(d):
        j = lax.rem(chip + d, n)
        return (2 * (j // nl) + core, lax.rem(j, nl))

    def columns(at):
        return (slice(None), pl.ds(pl.multiple_of(at * own, 128), own))

    def to_twin(h):
        to = (dp, twin(h))
        return (
            remote(wg_ref.at[label], wg_ref.at[label], wt_s.at[h], wt_r.at[h], to),
            remote(mg_ref.at[columns(label)], mg_ref.at[columns(label)], mt_s.at[h], mt_r.at[h], to),
        )

    half_lanes = wg_ref.shape[2] // 2
    half_block = block // 2

    def to_fellow(t, j):
        at = twin(sets - t // 2)
        to = (dp, fellow(j))
        w_part = wg_ref.at[at, :, pl.ds(pl.multiple_of(lax.rem(t, 2) * half_lanes, 128), half_lanes)]
        m_part = mg_ref.at[
            pl.ds(pl.multiple_of(lax.rem(t, 2) * half_block, 16), half_block),
            pl.ds(pl.multiple_of(at * own, 128), own),
        ]
        return (
            remote(w_part, w_part, wf_s.at[t], wf_r.at[t], to),
            remote(m_part, m_part, mf_s.at[t], mf_r.at[t], to),
        )

    def from_fellows(t):
        return (
            total_wait(wg_ref.at[pl.ds(0, 3), :, pl.ds(0, half_lanes)], wf_s.at[t], wf_r.at[t]),
            total_wait(mg_ref.at[pl.ds(0, half_block), pl.ds(0, 3 * own)], mf_s.at[t], mf_r.at[t]),
        )

    def tell_fellows(t):
        loop(1, 4, lambda j: [copy.start() for copy in to_fellow(t, j)])

    def pair(c):
        return remote(x_ref.at[c, away_rows], pbuf.at[c], pair_s.at[c], pair_r.at[c], partner)

    def forward(c):
        ref = vb.at[c, half_rows16]
        return remote(ref, ref, fw_s.at[c], fw_r.at[c], partner)

    def forward_ab():
        ref = ab.at[half_rows]
        return remote(ref, ref, abf_s, abf_r, partner)

    def total_wait(ref, send, recv):
        return remote(ref, ref, send, recv, partner)

    barrier = pltpu.get_barrier_semaphore()
    pl.semaphore_signal(barrier, inc=1, device_id=partner, device_id_type=MESH)
    loop(1, n, lambda d: pl.semaphore_signal(barrier, inc=1, device_id=chip_device(d), device_id_type=MESH))

    def product(lhs, terms, c):
        out = jnp.dot(lhs, c_ref[:, lanes(c)], preferred_element_type=f32)
        x_ref[c] = out[:block] + out[block:] if terms == 2 else out

    def scatter(c):
        pair(c).wait_recv()

        def send(d):
            e = MEMBERS - 1 - d
            to, g = member(e)
            sbuf[c, e] = x_ref[c, rows8(core, g)] + pbuf[c, pl.ds(pl.multiple_of(g * 8, 8), 8)]
            remote(sbuf.at[c, e], rbuf.at[c, e], rs_s.at[c], rs_r.at[c], to).start()

        loop(0, peers, send)

    def cross(c, par):
        acc = x_ref[c, mine] + pbuf[c, pl.ds(pl.multiple_of(me * 8, 8), 8)]
        total_wait(rbuf.at[c, pl.ds(1, peers)], rs_s.at[c], rs_r.at[c]).wait_recv()
        for e in range(1, MEMBERS):
            acc = acc + rbuf[c, e]
        stbuf[par, c, group] = acc
        ref = stbuf.at[par, c, group]
        loop(1, groups, lambda h: remote(ref, ref, st_s.at[par, c], st_r.at[par, c], other(h)).start())

    def crossed(c, par, first):
        if groups > 1:
            total_wait(stbuf.at[par, c, pl.ds(0, groups - 1)], st_s.at[par, c], st_r.at[par, c]).wait_recv()
        acc = stbuf[par, c, 0]
        for h in range(1, groups):
            acc = acc + stbuf[par, c, h]
        if first:
            acc = acc / diag_ref[...]
        direction = ds[:, lanes(c)]
        image = scale * acc + damp_ref[0:8, 0:1] * direction
        img[:, lanes(c)] = image
        vb[c, rows16(core, me)] = two_terms(image * inv[:, lanes(c)])

        def send(d):
            to, g = member(MEMBERS - 1 - d)
            ref = vb.at[c, rows16(core, me)]
            remote(ref, ref, ag_s.at[c], ag_r.at[c], to).start()

        loop(0, peers, send)
        return jnp.sum(direction * image, axis=1, keepdims=True)

    def rescale(curve):
        rho = rho_ref[:, 0:1]
        alpha = rho / curve
        fresh = jnp.zeros((8, 1), f32)
        for c in range(CHUNKS):
            resid = rs[:, lanes(c)] - alpha * img[:, lanes(c)]
            rs[:, lanes(c)] = resid
            fresh = fresh + jnp.sum(resid * resid * inv[:, lanes(c)], axis=1, keepdims=True)
        beta = fresh / rho
        lane = lax.broadcasted_iota(jnp.int32, (8, 128), 1)
        ab[mine] = jnp.where(lane < 64, alpha, beta)

        def send(d):
            to, g = member(MEMBERS - 1 - d)
            remote(ab.at[mine], ab.at[mine], ab_s, ab_r, to).start()

        loop(0, peers, send)
        rho_ref[...] = jnp.broadcast_to(fresh, (8, 128))
        for c in range(CHUNKS):
            direction = ds[:, lanes(c)]
            xs[:, lanes(c)] = xs[:, lanes(c)] + alpha * direction
            ds[:, lanes(c)] = rs[:, lanes(c)] * inv[:, lanes(c)] + beta * direction

    def gather(c):
        total_wait(vb.at[c, pl.ds(0, peers * 16)], ag_s.at[c], ag_r.at[c]).wait_recv()
        forward(c).start()

    def applied(c):
        forward(c).wait_recv()
        return lax.dot_general(
            vb[c], c_ref[:, lanes(c)], (((1,), (1,)), ((), ())), preferred_element_type=f32
        )

    def finish_sends():
        for c in range(CHUNKS):
            total_wait(vb.at[c, pl.ds(0, peers * 16)], ag_s.at[c], ag_r.at[c]).wait_send()
            forward(c).wait_send()
        total_wait(ab.at[pl.ds(0, peers * 8)], ab_s, ab_r).wait_send()
        forward_ab().wait_send()

    def reduce_and_apply(par, first, index):
        for c in range(CHUNKS):
            scatter(c)
        if first:
            share_stats()
        for c in range(CHUNKS):
            cross(c, par)
        if first:
            loop(1, sets, lambda h: [copy.start() for copy in to_twin(h)])
        for c in range(CHUNKS):
            pair(c).wait_send()
            total_wait(sbuf.at[c, pl.ds(1, peers)], rs_s.at[c], rs_r.at[c]).wait_send()
        if first:
            start_state()
        curve = jnp.zeros((8, 1), f32)
        for c in range(CHUNKS):
            curve = curve + crossed(c, par, first)
        rescale(curve)
        for c in range(CHUNKS):
            gather(c)
        total_wait(ab.at[pl.ds(0, peers * 8)], ab_s, ab_r).wait_recv()
        forward_ab().start()
        if not first:
            begin = (index - 1) * share
            loop(begin, jnp.minimum(begin + share, 2 * sets), tell_fellows)
        if groups > 1:
            for c in range(CHUNKS):
                total_wait(stbuf.at[par, c, pl.ds(0, groups - 1)], st_s.at[par, c], st_r.at[par, c]).wait_send()
        out = applied(0)
        for c in range(1, CHUNKS):
            out = out + applied(c)
        forward_ab().wait_recv()
        out = out.reshape(2 * block // 16, 2, 8, out.shape[1])
        out = (out[:, 0] + out[:, 1]).reshape(block, out.shape[3])
        applied_z = cz[...] - ab[:, 0:1] * out
        cz[...] = applied_z
        inner[...] = applied_z + ab[:, 64:65] * inner[...]

    local_stat, near_stat, member_stat, group_stat = 0, 1, 2, 2 + MEMBERS

    def pair_stats():
        return remote(stat.at[local_stat], stat.at[near_stat], sp_s, sp_r, partner)

    def share_stats():
        pair_stats().wait_recv()
        stat[member_stat + me] = stat[local_stat] + stat[near_stat]
        ref = stat.at[member_stat + me]
        loop(1, MEMBERS, lambda e: remote(ref, ref, sm_s, sm_r, member(e)[0]).start())

    def start_state():
        total_wait(stat.at[pl.ds(member_stat, peers)], sm_s, sm_r).wait_recv()
        acc = stat[member_stat]
        for e in range(1, MEMBERS):
            acc = acc + stat[member_stat + e]
        stat[group_stat + group] = acc
        ref = stat.at[group_stat + group]
        loop(1, groups, lambda h: remote(ref, ref, sg_s, sg_r, other(h)).start())
        if groups > 1:
            total_wait(stat.at[pl.ds(group_stat, groups - 1)], sg_s, sg_r).wait_recv()
        acc = stat[group_stat]
        for h in range(1, groups):
            acc = acc + stat[group_stat + h]
        damping = damp_fraction * 2.0 * jnp.sum(
            jnp.sum(acc, axis=0, keepdims=True), axis=1, keepdims=True
        ) / (tokens * width)
        damp_ref[...] = jnp.broadcast_to(damping, damp_ref.shape)
        diag = scale * acc + damping
        inverse = 1.0 / diag
        for j in range(stat_rows):
            inv[:, j * 128 : (j + 1) * 128] = jnp.broadcast_to(inverse[j : j + 1, :], (8, 128))
        row = lax.broadcasted_iota(jnp.int32, (block, 128), 0)
        lane = lax.broadcasted_iota(jnp.int32, (block, 128), 1)
        every = jnp.sum(jnp.where(row == lane, diag[0:1, :], 0.0), axis=1, keepdims=True)
        row8 = lax.broadcasted_iota(jnp.int32, (8, 128), 0) + core * half + me * 8
        lane8 = lax.broadcasted_iota(jnp.int32, (8, 128), 1)
        unit = jnp.where(row8 == lane8, 1.0, 0.0)
        own_diag = jnp.sum(unit * diag[0:1, :], axis=1, keepdims=True)
        diag_ref[...] = own_diag
        rho_ref[...] = jnp.broadcast_to(1.0 / own_diag, (8, 128))
        rs[...] = jnp.zeros_like(rs)
        ds[...] = jnp.zeros_like(ds)
        xs[...] = jnp.zeros_like(xs)
        rs[:, 0:128] = unit
        ds[:, 0:128] = unit / own_diag
        scaled = cz[...] / every
        cz[...] = scaled
        inner[...] = scaled
        pair_stats().wait_send()
        total_wait(stat.at[pl.ds(member_stat, peers)], sm_s, sm_r).wait_send()
        if groups > 1:
            total_wait(stat.at[pl.ds(group_stat, groups - 1)], sg_s, sg_r).wait_send()

    share = -(-2 * sets // (steps - 1))

    def fetch(c):
        return pltpu.make_async_copy(calib_ref.at[:, lanes(c)], c_ref.at[:, lanes(c)], load.at[c])

    for c in range(CHUNKS):
        fetch(c).start()
    fetch_mask = pltpu.make_async_copy(m_ref, mask_ref, load.at[CHUNKS])
    fetch_weights = pltpu.make_async_copy(w_ref, wg_ref.at[label], load.at[CHUNKS + 1])
    fetch_mask.start()
    fetch_weights.start()
    one = jnp.where(
        lax.broadcasted_iota(jnp.int32, (block, 128), 0) == lax.broadcasted_iota(jnp.int32, (block, 128), 1), 1.0, 0.0
    )
    fetch(0).wait()
    turned = lax.dot_general(
        one.astype(jnp.bfloat16), c_ref[:, 0:block], (((1,), (1,)), ((), ())), preferred_element_type=f32
    )
    cz[...] = turned
    lhs = turned.astype(jnp.bfloat16)
    product(lhs, 1, 0)
    pl.semaphore_wait(barrier, n)
    pair(0).start()
    for c in range(1, CHUNKS):
        fetch(c).wait()
        product(lhs, 1, c)
        pair(c).start()
    stat[local_stat] = jnp.zeros(stat.shape[1:], f32)
    for j in range(stat_rows):
        square = c_ref[:, j * 128 : (j + 1) * 128].astype(f32)
        stat[local_stat, j : j + 1, :] = jnp.sum(square * square, axis=0, keepdims=True)
    pair_stats().start()
    fetch_mask.wait()
    mg_ref[columns(label)] = mask_ref[...].astype(f32).T.astype(jnp.bfloat16)
    fetch_weights.wait()
    reduce_and_apply(0, True, 0)
    loop(1, sets, lambda h: [copy.wait_recv() for copy in to_twin(h)])

    def iteration(index, carry):
        lhs = two_terms(inner[...])
        for c in range(CHUNKS):
            product(lhs, 2, c)
            pair(c).start()
        finish_sends()
        reduce_and_apply(lax.rem(index, 2), False, index)
        return carry

    lax.fori_loop(1, steps, iteration, 0)

    energy = inner[...]
    local_ref[...] = lax.dot_general(
        jnp.ones((8, energy.shape[1]), f32),
        energy * energy,
        (((1,), (1,)), ((), ())),
        precision=lax.Precision.HIGHEST,
        preferred_element_type=f32,
    )
    near = remote(local_ref, part, e_s, e_r, partner)
    near.start()
    near_own = pl.ds(pl.multiple_of(core * half + me * 8, 8), 8)

    def message(at):
        begin = pl.multiple_of(window_start(at, block, cols, window, width), 128)
        view = pl.ds(begin, window)
        return begin, view

    lane8 = lax.broadcasted_iota(jnp.int32, (8, 128), 1)
    power = jnp.sum(ds[...] * ds[...], axis=1, keepdims=True)
    facts = jnp.where(lane8 < 64, rho_ref[...], power)

    def fill(ref, at, place_):
        begin, view = message(at)
        ref[place_ + (slice(0, 128),)] = xs[:, 0:128]
        ref[place_ + (slice(128, 128 + window),)] = xs[:, view]
        ref[place_ + (slice(128 + window, 256 + window),)] = ds[:, 0:128]
        ref[place_ + (slice(256 + window, 256 + 2 * window),)] = ds[:, view]
        ref[place_ + (slice(256 + 2 * window, 384 + 2 * window),)] = facts

    def tell(d):
        e = MEMBERS - 1 - d
        to, g = member(e)
        fill(gs, to[1], (e, slice(None)))
        remote(gs.at[e], gb.at[mine], g_s, g_r, to).start()

    near.wait_recv()
    slots[chip] = local_ref[...] + part[...]

    def far(d, j):
        return remote(slots.at[j], slots.at[j], en_s, en_r, chip_device(d))

    loop(1, n, lambda d: far(d, chip).start())
    loop(0, peers, tell)
    fill(gb, label, (near_own,))
    finish_sends()
    loop(1, sets, lambda h: [copy.wait_send() for copy in to_twin(h)])
    loop(0, 2 * sets, lambda t: [copy.wait_send() for copy in from_fellows(t)])
    loop(0, 2 * sets, lambda t: [copy.wait_recv() for copy in from_fellows(t)])
    total_wait(slots.at[pl.ds(0, n - 1)], en_s, en_r).wait_recv()
    norms = lax.fori_loop(1, n, lambda j, acc: acc + slots[j], slots[0])
    total_wait(gb.at[pl.ds(0, peers * 8)], g_s, g_r).wait_recv()
    last = remote(gb.at[half_rows], gb.at[half_rows], gf_s, gf_r, partner)
    last.start()
    near.wait_send()
    total_wait(slots.at[pl.ds(0, n - 1)], en_s, en_r).wait_send()
    total_wait(gs.at[pl.ds(1, peers)], g_s, g_r).wait_send()
    last.wait_recv()
    curve = scale * jnp.sum(one * norms[0:1, :], axis=1, keepdims=True)
    rho = gb[:, 256 + 2 * window : 257 + 2 * window]
    power = gb[:, 320 + 2 * window : 321 + 2 * window]
    alpha = rho / (curve + damp_ref[0:1, 0:1] * power)
    top_ref[...] = gb[:, 0:128] + alpha * gb[:, 128 + window : 256 + window]
    win_ref[...] = gb[:, 128 : 128 + window] + alpha * gb[:, 256 + window : 256 + 2 * window]
    last.wait_send()


def conjugate_gradients(calib, w, mask, block, cols, tokens, nd, nl):
    width = calib.shape[1]
    window = window_width(block, cols, nl)
    nx = math.isqrt(nl // 2)
    groups = (nx // 2) * (nd // 4) * (nl // nx // 2)
    sets = (nx // 2) * (nl // nx // 2)
    n = nd // 2 * nl
    chunk = width // CHUNKS
    f32, bf16 = jnp.float32, jnp.bfloat16
    vmem = pl.BlockSpec(memory_space=pltpu.VMEM)
    dma = pltpu.SemaphoreType.DMA
    stat_rows = -(-(width // 128) // 8) * 8
    message = 384 + 2 * window
    return pl.pallas_call(
        functools.partial(cg_kernel, nd, nl, cols, tokens),
        out_shape=(
            jax.ShapeDtypeStruct((block, 128), f32),
            jax.ShapeDtypeStruct((block, window), f32),
            jax.ShapeDtypeStruct((nl,) + w.shape, w.dtype),
            jax.ShapeDtypeStruct((block, mask.shape[0] * nl), bf16),
        ),
        in_specs=[pl.BlockSpec(memory_space=pltpu.HBM)] * 3,
        out_specs=(vmem,) * 4,
        scratch_shapes=[
            pltpu.VMEM(calib.shape, bf16),
            pltpu.VMEM(mask.shape, mask.dtype),
            pltpu.VMEM((CHUNKS, block, chunk), f32),
            pltpu.VMEM((CHUNKS, block // 2, chunk), f32),
            pltpu.VMEM((CHUNKS, MEMBERS, 8, chunk), f32),
            pltpu.VMEM((CHUNKS, MEMBERS, 8, chunk), f32),
            pltpu.VMEM((2, CHUNKS, groups, 8, chunk), f32),
            pltpu.VMEM((CHUNKS, 2 * block, chunk), bf16),
            pltpu.VMEM((block, 128), f32),
            pltpu.VMEM((8, width), f32),
            pltpu.VMEM((8, width), f32),
            pltpu.VMEM((8, width), f32),
            pltpu.VMEM((8, width), f32),
            pltpu.VMEM((8, width), f32),
            pltpu.VMEM((8, 128), f32),
            pltpu.VMEM((8, 1), f32),
            pltpu.VMEM((8, 128), f32),
            pltpu.VMEM((block, calib.shape[0]), f32),
            pltpu.VMEM((block, calib.shape[0]), f32),
            pltpu.VMEM((2 + MEMBERS + groups, stat_rows, 128), f32),
            pltpu.VMEM((MEMBERS, 8, message), f32),
            pltpu.VMEM((block, message), f32),
            pltpu.VMEM((8, block), f32),
            pltpu.VMEM((8, block), f32),
            pltpu.VMEM((n, 8, block), f32),
        ]
        + [dma((CHUNKS,))] * 4
        + [dma((2, CHUNKS))] * 2
        + [dma((CHUNKS,))] * 4
        + [dma] * 4
        + [dma] * 6
        + [dma] * 4
        + [dma] * 4
        + [dma((sets,))] * 4
        + [dma((2 * sets,))] * 4
        + [dma((CHUNKS + 2,))],
        compiler_params=pltpu.CompilerParams(collective_id=0, has_side_effects=True, vmem_limit_bytes=48 << 20),
        name="conjugate_gradients",
    )(calib, w, mask)


def finish_kernel(w_ref, m_ref, top_ref, t_ref, rest_ref, kept_ref, out_ref, sym, lower, tri, scales, errors, kept):
    block, rows = w_ref.shape
    own = kept_ref.shape[0]
    cols = rest_ref.shape[0]
    width = tri.shape[1]
    f32, bf16 = jnp.float32, jnp.bfloat16
    group = 512 if rows % 512 == 0 else rows
    top = top_ref[...]
    sym[...] = 0.5 * (top + top.T)
    lower[...] = jnp.zeros_like(lower)
    errors[...] = jnp.zeros_like(errors)
    tri[...] = jnp.zeros_like(tri)
    row = lax.broadcasted_iota(jnp.int32, (sub_width, 128), 0)

    def wide(x, lanes):
        return jnp.concatenate([x] * (lanes // 128), axis=1)

    def split(x):
        high = x.astype(bf16)
        return high, (x - high.astype(f32)).astype(bf16)

    for begin in range(0, block, sub_width):
        at = slice(begin, begin + sub_width)
        target = jnp.concatenate([sym[at, :], t_ref[at, :]], axis=1)
        if begin:
            factor = lower[...].T[at, :]
            target = target - jnp.dot(
                factor, tri[...], precision=lax.Precision.HIGHEST, preferred_element_type=f32
            )
            high, low = split(factor)
            factors = jnp.concatenate(
                [jnp.concatenate([high, high], axis=1), jnp.concatenate([low, jnp.zeros_like(low)], axis=1)], axis=0
            )
        spread = [
            jnp.broadcast_to(target[:, begin + j : begin + j + 1], (sub_width, 128)) for j in range(sub_width)
        ]
        steps = []
        inverses = []
        for j in range(sub_width):
            inverse = 1.0 / spread[j][j : j + 1, :]
            step = jnp.where(row > j, spread[j] * inverse, 0.0)
            for k in range(j + 1, sub_width):
                spread[k] = spread[k] - step * spread[k][j : j + 1, :]
            steps.append(step)
            inverses.append(inverse)
        for j in range(sub_width):
            target = target - wide(steps[j], width) * target[j : j + 1, :]
        tri[at, :] = target
        inverse = jnp.concatenate(inverses, axis=0)
        scales[at, :] = inverse
        lower[at, :] = target[:, :block] * inverse
        for first in range(0, rows, group):
            lanes = slice(first, first + group)
            window = w_ref[at, lanes].astype(f32)
            chosen = m_ref[at, lanes].astype(f32)
            if begin:
                both = jnp.dot(factors, errors[:, lanes], preferred_element_type=f32)
                window = window - (both[:sub_width] + both[sub_width:])
            for j in range(sub_width):
                window = window - wide(steps[j], group) * (chosen[j : j + 1, :] * window[j : j + 1, :])
            error = chosen * window
            high, low = split(error)
            errors[at, lanes] = high
            errors[slice(block + begin, block + begin + sub_width), lanes] = low
            kept[at, lanes] = window - error
    label = lax.axis_index("label")
    kept_ref[...] = kept[:, pl.ds(pl.multiple_of(label * own, 128), own)].T.astype(kept_ref.dtype)
    cross = (tri[:, 128:] * wide(scales[...], width - 128)).T[:cols]
    high, low = split(cross)
    twice = jnp.concatenate([high, high], axis=1)
    for first in range(0, rows, group):
        lanes = slice(first, first + group)
        delta = jnp.dot(twice, errors[:, lanes], preferred_element_type=f32)
        delta = delta + jnp.dot(low, errors[:block, lanes], preferred_element_type=f32)
        out_ref[:, lanes] = (rest_ref[:, lanes].astype(f32) - delta).astype(out_ref.dtype)


def finish(weights, mask, top, target, rest, own):
    block, rows = weights.shape
    cols = rest.shape[0]
    f32, bf16 = jnp.float32, jnp.bfloat16
    padded = -(-cols // 128) * 128
    target = jnp.pad(target, ((0, 0), (0, padded - cols)))
    vmem = pl.BlockSpec(memory_space=pltpu.VMEM)
    return pl.pallas_call(
        finish_kernel,
        out_shape=(jax.ShapeDtypeStruct((own, block), bf16), jax.ShapeDtypeStruct((cols, rows), bf16)),
        in_specs=[vmem] * 5,
        out_specs=(vmem, vmem),
        scratch_shapes=[
            pltpu.VMEM((block, block), f32),
            pltpu.VMEM((block, block), f32),
            pltpu.VMEM((block, 128 + padded), f32),
            pltpu.VMEM((block, 128), f32),
            pltpu.VMEM((2 * block, rows), bf16),
            pltpu.VMEM((block, rows), f32),
        ],
        compiler_params=pltpu.CompilerParams(vmem_limit_bytes=48 << 20),
        name="finish",
    )(weights, mask, top, target, rest)


def per_device(calib, block_weight, rest_weight, prune_mask):
    block = prune_mask.shape[1]
    nd, nl = lax.axis_size("dp"), lax.axis_size("label")
    own = prune_mask.shape[0]
    label = lax.axis_index("label")
    width = calib.shape[1]
    rest_cols = rest_weight.shape[1]
    top, near, weights, mask = conjugate_gradients(
        calib,
        block_weight.T,
        prune_mask,
        block,
        rest_cols,
        calib.shape[0] * nd * nl,
        nd,
        nl,
    )
    weights = weights.reshape(block, -1)
    begin = window_start(label, block, rest_cols, near.shape[1], width)
    owned = lax.dynamic_slice_in_dim(near, block + label * rest_cols - begin, rest_cols, 1)
    pruned_block, updated_rest = finish(weights, mask, top, owned, rest_weight.T, own)
    return (pruned_block, updated_rest.T)


def solution(mesh):
    return jax.shard_map(
        per_device,
        mesh=mesh,
        in_specs=(
            P(("dp", "label"), None),
            P("dp", "label"),
            P("dp", "label"),
            P(("dp", "label"), None),
        ),
        out_specs=(P(("dp", "label"), None), P("dp", "label")),
        check_vma=False,
    )
```

```python
import functools
import math

import jax
import jax.numpy as jnp
from jax import lax
from jax.experimental import pallas as pl
from jax.experimental.pallas import tpu as pltpu
from jax.sharding import PartitionSpec as P

ITERS = 6
MESH = pl.DeviceIdType.MESH

damp_fraction = 0.01
sub_width = 16
CHUNKS = 7
MEMBERS = 8


def two_terms(x):
    high = x.astype(jnp.bfloat16)
    low = (x - high.astype(jnp.float32)).astype(jnp.bfloat16)
    return jnp.concatenate([high, low], axis=0)


def loop(low, high, body):
    def step(d, carry):
        body(d)
        return carry

    lax.fori_loop(low, high, step, 0)


def remote(src, dst, send, recv, to):
    return pltpu.make_async_remote_copy(
        src_ref=src, dst_ref=dst, send_sem=send, recv_sem=recv, device_id=to, device_id_type=MESH
    )


def window_start(label, block, cols, window, width):
    return jnp.minimum((block + label * cols) // 128, (width - window) // 128) * 128


def window_width(block, cols, nl):
    return max(-(-((block + at * cols) % 128 + cols) // 128) * 128 for at in range(nl))


def place(nd, nl):
    nx = math.isqrt(nl // 2)
    ny, nz = nd // 2, nl // nx
    groups = (nx // 2) * (ny // 2) * (nz // 2)
    dp = lax.axis_index("dp")
    label = lax.axis_index("label")
    core, y, z, x = lax.rem(dp, 2), dp // 2, label // nx, lax.rem(label, nx)
    mx, my, mz = lax.rem(x, 2), lax.rem(y, 2), lax.rem(z, 2)
    qx, qy, qz = x // 2, y // 2, z // 2
    group = (qz * (ny // 2) + qy) * (nx // 2) + qx

    def member(e):
        hx, hy, hz = lax.rem(mx + lax.rem(e, 2), 2), lax.rem(my + lax.rem(e // 2, 2), 2), lax.rem(mz + e // 4, 2)
        return ((qy * 2 + hy) * 2 + core, (qz * 2 + hz) * nx + qx * 2 + hx), hz * 4 + hy * 2 + hx

    def other(h):
        q = lax.rem(group + h, groups)
        hx, hy, hz = lax.rem(q, nx // 2), lax.rem(q // (nx // 2), ny // 2), q // ((nx // 2) * (ny // 2))
        return ((hy * 2 + my) * 2 + core, (hz * 2 + mz) * nx + hx * 2 + mx)

    sets = (nx // 2) * (nz // 2)
    here = qz * (nx // 2) + qx

    def twin(h):
        q = lax.rem(here + h, sets)
        return (q // (nx // 2) * 2 + mz) * nx + lax.rem(q, nx // 2) * 2 + mx

    def fellow(j):
        return (qz * 2 + lax.rem(mz + j // 2, 2)) * nx + qx * 2 + lax.rem(mx + lax.rem(j, 2), 2)

    partner = (dp + 1 - 2 * core, label)
    return core, mz * 4 + my * 2 + mx, group, groups, member, other, partner, sets, twin, fellow


def cg_kernel(
    nd, nl, cols, tokens, calib_ref, w_ref, m_ref, top_ref, win_ref, wg_ref, mg_ref,
    c_ref, mask_ref, x_ref, pbuf, sbuf, rbuf, stbuf, vb, ab, img, xs, rs, ds, inv, damp_ref, diag_ref, rho_ref,
    cz, inner, stat, gs, gb, local_ref, part, slots,
    pair_s, pair_r, rs_s, rs_r, st_s, st_r, ag_s, ag_r, fw_s, fw_r, ab_s, ab_r, abf_s, abf_r,
    sp_s, sp_r, sm_s, sm_r, sg_s, sg_r, g_s, g_r, gf_s, gf_r, e_s, e_r, en_s, en_r, wt_s, wt_r, mt_s, mt_r, wf_s, wf_r, mf_s, mf_r, load,
):
    block = top_ref.shape[0]
    width = c_ref.shape[1]
    window = win_ref.shape[1]
    chunk = width // CHUNKS
    half = block // 2
    peers = MEMBERS - 1
    stat_rows = width // 128
    steps = ITERS - 1
    f32 = jnp.float32
    scale = 2.0 / tokens
    core, me, group, groups, member, other, partner, sets, twin, fellow = place(nd, nl)
    dp = lax.axis_index("dp")
    label = lax.axis_index("label")
    n = (nd // 2) * nl
    chip = (dp // 2) * nl + label
    own = m_ref.shape[0]

    def lanes(c):
        return pl.ds(c * chunk, chunk)

    def rows8(core_, g):
        return pl.ds(pl.multiple_of(core_ * half + g * 8, 8), 8)

    def rows16(core_, g):
        return pl.ds(pl.multiple_of(core_ * 2 * half + g * 16, 16), 16)

    half_rows = pl.ds(pl.multiple_of(core * half, half), half)
    away_rows = pl.ds(pl.multiple_of((1 - core) * half, half), half)
    half_rows16 = pl.ds(pl.multiple_of(core * 2 * half, 2 * half), 2 * half)
    mine = rows8(core, me)

    def chip_device(d):
        j = lax.rem(chip + d, n)
        return (2 * (j // nl) + core, lax.rem(j, nl))

    def columns(at):
        return (slice(None), pl.ds(pl.multiple_of(at * own, 128), own))

    def to_twin(h):
        to = (dp, twin(h))
        return (
            remote(wg_ref.at[label], wg_ref.at[label], wt_s.at[h], wt_r.at[h], to),
            remote(mg_ref.at[columns(label)], mg_ref.at[columns(label)], mt_s.at[h], mt_r.at[h], to),
        )

    half_lanes = wg_ref.shape[2] // 2
    half_block = block // 2

    def to_fellow(t, j):
        at = twin(sets - t // 2)
        to = (dp, fellow(j))
        w_part = wg_ref.at[at, :, pl.ds(pl.multiple_of(lax.rem(t, 2) * half_lanes, 128), half_lanes)]
        m_part = mg_ref.at[
            pl.ds(pl.multiple_of(lax.rem(t, 2) * half_block, 16), half_block),
            pl.ds(pl.multiple_of(at * own, 128), own),
        ]
        return (
            remote(w_part, w_part, wf_s.at[t], wf_r.at[t], to),
            remote(m_part, m_part, mf_s.at[t], mf_r.at[t], to),
        )

    def from_fellows(t):
        return (
            total_wait(wg_ref.at[pl.ds(0, 3), :, pl.ds(0, half_lanes)], wf_s.at[t], wf_r.at[t]),
            total_wait(mg_ref.at[pl.ds(0, half_block), pl.ds(0, 3 * own)], mf_s.at[t], mf_r.at[t]),
        )

    def tell_fellows(t):
        loop(1, 4, lambda j: [copy.start() for copy in to_fellow(t, j)])

    def pair(c):
        return remote(x_ref.at[c, away_rows], pbuf.at[c], pair_s.at[c], pair_r.at[c], partner)

    def forward(c):
        ref = vb.at[c, half_rows16]
        return remote(ref, ref, fw_s.at[c], fw_r.at[c], partner)

    def forward_ab():
        ref = ab.at[half_rows]
        return remote(ref, ref, abf_s, abf_r, partner)

    def total_wait(ref, send, recv):
        return remote(ref, ref, send, recv, partner)

    barrier = pltpu.get_barrier_semaphore()
    pl.semaphore_signal(barrier, inc=1, device_id=partner, device_id_type=MESH)
    loop(1, n, lambda d: pl.semaphore_signal(barrier, inc=1, device_id=chip_device(d), device_id_type=MESH))

    def product(lhs, terms, c):
        out = jnp.dot(lhs, c_ref[:, lanes(c)], preferred_element_type=f32)
        x_ref[c] = out[:block] + out[block:] if terms == 2 else out

    def scatter(c):
        pair(c).wait_recv()

        def send(d):
            e = MEMBERS - 1 - d
            to, g = member(e)
            sbuf[c, e] = x_ref[c, rows8(core, g)] + pbuf[c, pl.ds(pl.multiple_of(g * 8, 8), 8)]
            remote(sbuf.at[c, e], rbuf.at[c, e], rs_s.at[c], rs_r.at[c], to).start()

        loop(0, peers, send)

    def cross(c, par):
        acc = x_ref[c, mine] + pbuf[c, pl.ds(pl.multiple_of(me * 8, 8), 8)]
        total_wait(rbuf.at[c, pl.ds(1, peers)], rs_s.at[c], rs_r.at[c]).wait_recv()
        for e in range(1, MEMBERS):
            acc = acc + rbuf[c, e]
        stbuf[par, c, group] = acc
        ref = stbuf.at[par, c, group]
        loop(1, groups, lambda h: remote(ref, ref, st_s.at[par, c], st_r.at[par, c], other(h)).start())

    def total_image(c, par, first):
        if groups > 1:
            total_wait(stbuf.at[par, c, pl.ds(0, groups - 1)], st_s.at[par, c], st_r.at[par, c]).wait_recv()
        acc = stbuf[par, c, 0]
        for h in range(1, groups):
            acc = acc + stbuf[par, c, h]
        if first:
            acc = acc / diag_ref[...]
        direction = ds[:, lanes(c)]
        image = scale * acc + damp_ref[0:8, 0:1] * direction
        img[:, lanes(c)] = image
        return image * inv[:, lanes(c)], jnp.sum(direction * image, axis=1, keepdims=True)

    def publish(slot, terms):
        vb[slot, rows16(core, me)] = terms

        def send(d):
            to, g = member(MEMBERS - 1 - d)
            ref = vb.at[slot, rows16(core, me)]
            remote(ref, ref, ag_s.at[slot], ag_r.at[slot], to).start()

        loop(0, peers, send)

    def publish_all(par, first, last):
        curve = jnp.zeros((8, 1), f32)
        held = None
        for c in range(CHUNKS):
            term, part_curve = total_image(c, par, first)
            curve = curve + part_curve
            if not last:
                publish(c, two_terms(term))
            elif held is None and c + 1 < CHUNKS:
                held = term
            else:
                both = [term, jnp.zeros_like(term)] if held is None else [held, term]
                publish(c // 2, jnp.concatenate(both, axis=0).astype(jnp.bfloat16))
                held = None
        return curve

    def rescale(curve):
        rho = rho_ref[:, 0:1]
        alpha = rho / curve
        fresh = jnp.zeros((8, 1), f32)
        for c in range(CHUNKS):
            resid = rs[:, lanes(c)] - alpha * img[:, lanes(c)]
            rs[:, lanes(c)] = resid
            fresh = fresh + jnp.sum(resid * resid * inv[:, lanes(c)], axis=1, keepdims=True)
        beta = fresh / rho
        lane = lax.broadcasted_iota(jnp.int32, (8, 128), 1)
        ab[mine] = jnp.where(lane < 64, alpha, beta)

        def send(d):
            to, g = member(MEMBERS - 1 - d)
            remote(ab.at[mine], ab.at[mine], ab_s, ab_r, to).start()

        loop(0, peers, send)
        rho_ref[...] = jnp.broadcast_to(fresh, (8, 128))
        for c in range(CHUNKS):
            direction = ds[:, lanes(c)]
            xs[:, lanes(c)] = xs[:, lanes(c)] + alpha * direction
            ds[:, lanes(c)] = rs[:, lanes(c)] * inv[:, lanes(c)] + beta * direction

    def gather(c):
        total_wait(vb.at[c, pl.ds(0, peers * 16)], ag_s.at[c], ag_r.at[c]).wait_recv()
        forward(c).start()

    def times_calib(slot, c):
        return lax.dot_general(
            vb[slot], c_ref[:, lanes(c)], (((1,), (1,)), ((), ())), preferred_element_type=f32
        )

    def applied(slots, last):
        one_term, other_term = None, None
        for slot in range(slots):
            forward(slot).wait_recv()
            if not last:
                out = times_calib(slot, slot)
                one_term = out if one_term is None else one_term + out
            else:
                out = times_calib(slot, 2 * slot)
                one_term = out if one_term is None else one_term + out
                if 2 * slot + 1 < CHUNKS:
                    out = times_calib(slot, 2 * slot + 1)
                    other_term = out if other_term is None else other_term + out
        if other_term is None:
            other_term = one_term
        one_term = one_term.reshape(2 * block // 16, 2, 8, one_term.shape[1])
        other_term = other_term.reshape(one_term.shape)
        return (one_term[:, 0] + other_term[:, 1]).reshape(block, one_term.shape[3])

    def finish_sends(slots=CHUNKS):
        for c in range(slots):
            total_wait(vb.at[c, pl.ds(0, peers * 16)], ag_s.at[c], ag_r.at[c]).wait_send()
            forward(c).wait_send()
        total_wait(ab.at[pl.ds(0, peers * 8)], ab_s, ab_r).wait_send()
        forward_ab().wait_send()

    def message(at):
        return pl.ds(pl.multiple_of(window_start(at, block, cols, window, width), 128), window)

    def fill(ref, at, where, facts):
        view = message(at)
        ref[where + (slice(0, 128),)] = xs[:, 0:128]
        ref[where + (slice(128, 128 + window),)] = xs[:, view]
        ref[where + (slice(128 + window, 256 + window),)] = ds[:, 0:128]
        ref[where + (slice(256 + window, 256 + 2 * window),)] = ds[:, view]
        ref[where + (slice(256 + 2 * window, 384 + 2 * window),)] = facts

    def tell_all():
        lane8 = lax.broadcasted_iota(jnp.int32, (8, 128), 1)
        power = jnp.sum(ds[...] * ds[...], axis=1, keepdims=True)
        facts = jnp.where(lane8 < 64, rho_ref[...], power)

        def tell(d):
            e = MEMBERS - 1 - d
            to, g = member(e)
            fill(gs, to[1], (e, slice(None)), facts)
            remote(gs.at[e], gb.at[mine], g_s, g_r, to).start()

        loop(0, peers, tell)
        fill(gb, label, (mine,), facts)

    def reduce_and_apply(par, first, last, index):
        for c in range(CHUNKS):
            scatter(c)
            if first and c == 0:
                share_stats()
        for c in range(CHUNKS):
            cross(c, par)
            if first and c == 0:
                cross_stats()
        if first:
            loop(1, sets, lambda h: [copy.start() for copy in to_twin(h)])
        for c in range(CHUNKS):
            pair(c).wait_send()
            total_wait(sbuf.at[c, pl.ds(1, peers)], rs_s.at[c], rs_r.at[c]).wait_send()
        if first:
            start_state()
        rescale(publish_all(par, first, last))
        if last:
            tell_all()
        slots = -(-CHUNKS // 2) if last else CHUNKS
        for slot in range(slots):
            gather(slot)
        total_wait(ab.at[pl.ds(0, peers * 8)], ab_s, ab_r).wait_recv()
        forward_ab().start()
        if not first:
            begin = (index - 1) * share
            loop(begin, jnp.minimum(begin + share, 2 * sets), tell_fellows)
        if groups > 1:
            for c in range(CHUNKS):
                total_wait(stbuf.at[par, c, pl.ds(0, groups - 1)], st_s.at[par, c], st_r.at[par, c]).wait_send()
        out = applied(slots, last)
        forward_ab().wait_recv()
        applied_z = cz[...] - ab[:, 0:1] * out
        cz[...] = applied_z
        inner[...] = applied_z + ab[:, 64:65] * inner[...]

    def begin_step(lhs, terms):
        for c in range(CHUNKS):
            product(lhs, terms, c)
            pair(c).start()

    local_stat, near_stat, member_stat, group_stat = 0, 1, 2, 2 + MEMBERS

    def pair_stats():
        return remote(stat.at[local_stat], stat.at[near_stat], sp_s, sp_r, partner)

    def share_stats():
        pair_stats().wait_recv()
        stat[member_stat + me] = stat[local_stat] + stat[near_stat]
        ref = stat.at[member_stat + me]
        loop(1, MEMBERS, lambda e: remote(ref, ref, sm_s, sm_r, member(e)[0]).start())

    def cross_stats():
        total_wait(stat.at[pl.ds(member_stat, peers)], sm_s, sm_r).wait_recv()
        acc = stat[member_stat]
        for e in range(1, MEMBERS):
            acc = acc + stat[member_stat + e]
        stat[group_stat + group] = acc
        ref = stat.at[group_stat + group]
        loop(1, groups, lambda h: remote(ref, ref, sg_s, sg_r, other(h)).start())

    def start_state():
        if groups > 1:
            total_wait(stat.at[pl.ds(group_stat, groups - 1)], sg_s, sg_r).wait_recv()
        acc = stat[group_stat]
        for h in range(1, groups):
            acc = acc + stat[group_stat + h]
        damping = damp_fraction * 2.0 * jnp.sum(
            jnp.sum(acc, axis=0, keepdims=True), axis=1, keepdims=True
        ) / (tokens * width)
        damp_ref[...] = jnp.broadcast_to(damping, damp_ref.shape)
        diag = scale * acc + damping
        inverse = 1.0 / diag
        for j in range(stat_rows):
            inv[:, j * 128 : (j + 1) * 128] = jnp.broadcast_to(inverse[j : j + 1, :], (8, 128))
        row = lax.broadcasted_iota(jnp.int32, (block, 128), 0)
        lane = lax.broadcasted_iota(jnp.int32, (block, 128), 1)
        every = jnp.sum(jnp.where(row == lane, diag[0:1, :], 0.0), axis=1, keepdims=True)
        row8 = lax.broadcasted_iota(jnp.int32, (8, 128), 0) + core * half + me * 8
        lane8 = lax.broadcasted_iota(jnp.int32, (8, 128), 1)
        unit = jnp.where(row8 == lane8, 1.0, 0.0)
        own_diag = jnp.sum(unit * diag[0:1, :], axis=1, keepdims=True)
        diag_ref[...] = own_diag
        rho_ref[...] = jnp.broadcast_to(1.0 / own_diag, (8, 128))
        rs[...] = jnp.zeros_like(rs)
        ds[...] = jnp.zeros_like(ds)
        xs[...] = jnp.zeros_like(xs)
        rs[:, 0:128] = unit
        ds[:, 0:128] = unit / own_diag
        scaled = cz[...] / every
        cz[...] = scaled
        inner[...] = scaled
        pair_stats().wait_send()
        total_wait(stat.at[pl.ds(member_stat, peers)], sm_s, sm_r).wait_send()
        if groups > 1:
            total_wait(stat.at[pl.ds(group_stat, groups - 1)], sg_s, sg_r).wait_send()

    share = -(-2 * sets // (steps - 1))

    def fetch(c):
        return pltpu.make_async_copy(calib_ref.at[:, lanes(c)], c_ref.at[:, lanes(c)], load.at[c])

    for c in range(CHUNKS):
        fetch(c).start()
    fetch_mask = pltpu.make_async_copy(m_ref, mask_ref, load.at[CHUNKS])
    fetch_weights = pltpu.make_async_copy(w_ref, wg_ref.at[label], load.at[CHUNKS + 1])
    fetch_mask.start()
    fetch_weights.start()
    one = jnp.where(
        lax.broadcasted_iota(jnp.int32, (block, 128), 0) == lax.broadcasted_iota(jnp.int32, (block, 128), 1), 1.0, 0.0
    )
    fetch(0).wait()
    turned = lax.dot_general(
        one.astype(jnp.bfloat16), c_ref[:, 0:block], (((1,), (1,)), ((), ())), preferred_element_type=f32
    )
    cz[...] = turned
    lhs = turned.astype(jnp.bfloat16)
    product(lhs, 1, 0)
    stat[local_stat] = jnp.zeros(stat.shape[1:], f32)
    for c in range(CHUNKS):
        if c:
            fetch(c).wait()
        for j in range(c * chunk // 128, (c + 1) * chunk // 128):
            square = c_ref[:, j * 128 : (j + 1) * 128].astype(f32)
            stat[local_stat, j : j + 1, :] = jnp.sum(square * square, axis=0, keepdims=True)
    pl.semaphore_wait(barrier, n)
    pair_stats().start()
    pair(0).start()
    for c in range(1, CHUNKS):
        product(lhs, 1, c)
        pair(c).start()
    fetch_mask.wait()
    mg_ref[columns(label)] = mask_ref[...].astype(f32).T.astype(jnp.bfloat16)
    fetch_weights.wait()
    reduce_and_apply(0, True, False, 0)
    loop(1, sets, lambda h: [copy.wait_recv() for copy in to_twin(h)])

    def iteration(index, carry):
        begin_step(two_terms(inner[...]), 2)
        finish_sends()
        reduce_and_apply(lax.rem(index, 2), False, False, index)
        return carry

    lax.fori_loop(1, steps - 1, iteration, 0)
    begin_step(two_terms(inner[...]), 2)
    finish_sends()
    reduce_and_apply((steps - 1) % 2, False, True, steps - 1)
    energy = inner[...]
    local_ref[...] = lax.dot_general(
        jnp.ones((8, energy.shape[1]), f32),
        energy * energy,
        (((1,), (1,)), ((), ())),
        precision=lax.Precision.HIGHEST,
        preferred_element_type=f32,
    )
    near = remote(local_ref, part, e_s, e_r, partner)
    near.start()
    near.wait_recv()
    slots[chip] = local_ref[...] + part[...]

    def far(d, j):
        return remote(slots.at[j], slots.at[j], en_s, en_r, chip_device(d))

    loop(1, n, lambda d: far(d, chip).start())
    finish_sends(-(-CHUNKS // 2))
    loop(1, sets, lambda h: [copy.wait_send() for copy in to_twin(h)])
    loop(0, 2 * sets, lambda t: [copy.wait_send() for copy in from_fellows(t)])
    loop(0, 2 * sets, lambda t: [copy.wait_recv() for copy in from_fellows(t)])
    total_wait(slots.at[pl.ds(0, n - 1)], en_s, en_r).wait_recv()
    norms = lax.fori_loop(1, n, lambda j, acc: acc + slots[j], slots[0])
    total_wait(gb.at[pl.ds(0, peers * 8)], g_s, g_r).wait_recv()
    last = remote(gb.at[half_rows], gb.at[half_rows], gf_s, gf_r, partner)
    last.start()
    near.wait_send()
    total_wait(slots.at[pl.ds(0, n - 1)], en_s, en_r).wait_send()
    total_wait(gs.at[pl.ds(1, peers)], g_s, g_r).wait_send()
    last.wait_recv()
    curve = scale * jnp.sum(one * norms[0:1, :], axis=1, keepdims=True)
    rho = gb[:, 256 + 2 * window : 257 + 2 * window]
    power = gb[:, 320 + 2 * window : 321 + 2 * window]
    alpha = rho / (curve + damp_ref[0:1, 0:1] * power)
    top_ref[...] = gb[:, 0:128] + alpha * gb[:, 128 + window : 256 + window]
    win_ref[...] = gb[:, 128 : 128 + window] + alpha * gb[:, 256 + window : 256 + 2 * window]
    last.wait_send()


def conjugate_gradients(calib, w, mask, block, cols, tokens, nd, nl):
    width = calib.shape[1]
    window = window_width(block, cols, nl)
    nx = math.isqrt(nl // 2)
    groups = (nx // 2) * (nd // 4) * (nl // nx // 2)
    sets = (nx // 2) * (nl // nx // 2)
    n = nd // 2 * nl
    chunk = width // CHUNKS
    f32, bf16 = jnp.float32, jnp.bfloat16
    vmem = pl.BlockSpec(memory_space=pltpu.VMEM)
    dma = pltpu.SemaphoreType.DMA
    stat_rows = -(-(width // 128) // 8) * 8
    message = 384 + 2 * window
    return pl.pallas_call(
        functools.partial(cg_kernel, nd, nl, cols, tokens),
        out_shape=(
            jax.ShapeDtypeStruct((block, 128), f32),
            jax.ShapeDtypeStruct((block, window), f32),
            jax.ShapeDtypeStruct((nl,) + w.shape, w.dtype),
            jax.ShapeDtypeStruct((block, mask.shape[0] * nl), bf16),
        ),
        in_specs=[pl.BlockSpec(memory_space=pltpu.HBM)] * 3,
        out_specs=(vmem,) * 4,
        scratch_shapes=[
            pltpu.VMEM(calib.shape, bf16),
            pltpu.VMEM(mask.shape, mask.dtype),
            pltpu.VMEM((CHUNKS, block, chunk), f32),
            pltpu.VMEM((CHUNKS, block // 2, chunk), f32),
            pltpu.VMEM((CHUNKS, MEMBERS, 8, chunk), f32),
            pltpu.VMEM((CHUNKS, MEMBERS, 8, chunk), f32),
            pltpu.VMEM((2, CHUNKS, groups, 8, chunk), f32),
            pltpu.VMEM((CHUNKS, 2 * block, chunk), bf16),
            pltpu.VMEM((block, 128), f32),
            pltpu.VMEM((8, width), f32),
            pltpu.VMEM((8, width), f32),
            pltpu.VMEM((8, width), f32),
            pltpu.VMEM((8, width), f32),
            pltpu.VMEM((8, width), f32),
            pltpu.VMEM((8, 128), f32),
            pltpu.VMEM((8, 1), f32),
            pltpu.VMEM((8, 128), f32),
            pltpu.VMEM((block, calib.shape[0]), f32),
            pltpu.VMEM((block, calib.shape[0]), f32),
            pltpu.VMEM((2 + MEMBERS + groups, stat_rows, 128), f32),
            pltpu.VMEM((MEMBERS, 8, message), f32),
            pltpu.VMEM((block, message), f32),
            pltpu.VMEM((8, block), f32),
            pltpu.VMEM((8, block), f32),
            pltpu.VMEM((n, 8, block), f32),
        ]
        + [dma((CHUNKS,))] * 4
        + [dma((2, CHUNKS))] * 2
        + [dma((CHUNKS,))] * 4
        + [dma] * 4
        + [dma] * 6
        + [dma] * 4
        + [dma] * 4
        + [dma((sets,))] * 4
        + [dma((2 * sets,))] * 4
        + [dma((CHUNKS + 2,))],
        compiler_params=pltpu.CompilerParams(collective_id=0, has_side_effects=True, vmem_limit_bytes=48 << 20),
        name="conjugate_gradients",
    )(calib, w, mask)


def finish_kernel(w_ref, m_ref, top_ref, t_ref, rest_ref, kept_ref, out_ref, sym, lower, tri, scales, errors, kept):
    block, rows = w_ref.shape
    own = kept_ref.shape[0]
    cols = rest_ref.shape[0]
    width = tri.shape[1]
    f32, bf16 = jnp.float32, jnp.bfloat16
    group = 512 if rows % 512 == 0 else rows
    top = top_ref[...]
    sym[...] = 0.5 * (top + top.T)
    lower[...] = jnp.zeros_like(lower)
    errors[...] = jnp.zeros_like(errors)
    tri[...] = jnp.zeros_like(tri)
    row = lax.broadcasted_iota(jnp.int32, (sub_width, 128), 0)

    def wide(x, lanes):
        return jnp.concatenate([x] * (lanes // 128), axis=1)

    def split(x):
        high = x.astype(bf16)
        return high, (x - high.astype(f32)).astype(bf16)

    for begin in range(0, block, sub_width):
        at = slice(begin, begin + sub_width)
        target = jnp.concatenate([sym[at, :], t_ref[at, :]], axis=1)
        if begin:
            factor = lower[...].T[at, :]
            target = target - jnp.dot(
                factor, tri[...], precision=lax.Precision.HIGHEST, preferred_element_type=f32
            )
            high, low = split(factor)
            factors = jnp.concatenate(
                [jnp.concatenate([high, high], axis=1), jnp.concatenate([low, jnp.zeros_like(low)], axis=1)], axis=0
            )
        spread = [
            jnp.broadcast_to(target[:, begin + j : begin + j + 1], (sub_width, 128)) for j in range(sub_width)
        ]
        steps = []
        inverses = []
        for j in range(sub_width):
            inverse = 1.0 / spread[j][j : j + 1, :]
            step = jnp.where(row > j, spread[j] * inverse, 0.0)
            for k in range(j + 1, sub_width):
                spread[k] = spread[k] - step * spread[k][j : j + 1, :]
            steps.append(step)
            inverses.append(inverse)
        for j in range(sub_width):
            target = target - wide(steps[j], width) * target[j : j + 1, :]
        tri[at, :] = target
        inverse = jnp.concatenate(inverses, axis=0)
        scales[at, :] = inverse
        lower[at, :] = target[:, :block] * inverse
        for first in range(0, rows, group):
            lanes = slice(first, first + group)
            window = w_ref[at, lanes].astype(f32)
            chosen = m_ref[at, lanes].astype(f32)
            if begin:
                both = jnp.dot(factors, errors[:, lanes], preferred_element_type=f32)
                window = window - (both[:sub_width] + both[sub_width:])
            for j in range(sub_width):
                window = window - wide(steps[j], group) * (chosen[j : j + 1, :] * window[j : j + 1, :])
            error = chosen * window
            high, low = split(error)
            errors[at, lanes] = high
            errors[slice(block + begin, block + begin + sub_width), lanes] = low
            kept[at, lanes] = window - error
    label = lax.axis_index("label")
    kept_ref[...] = kept[:, pl.ds(pl.multiple_of(label * own, 128), own)].T.astype(kept_ref.dtype)
    cross = (tri[:, 128:] * wide(scales[...], width - 128)).T[:cols]
    high, low = split(cross)
    twice = jnp.concatenate([high, high], axis=1)
    for first in range(0, rows, group):
        lanes = slice(first, first + group)
        delta = jnp.dot(twice, errors[:, lanes], preferred_element_type=f32)
        delta = delta + jnp.dot(low, errors[:block, lanes], preferred_element_type=f32)
        out_ref[:, lanes] = (rest_ref[:, lanes].astype(f32) - delta).astype(out_ref.dtype)


def finish(weights, mask, top, target, rest, own):
    block, rows = weights.shape
    cols = rest.shape[0]
    f32, bf16 = jnp.float32, jnp.bfloat16
    padded = -(-cols // 128) * 128
    target = jnp.pad(target, ((0, 0), (0, padded - cols)))
    vmem = pl.BlockSpec(memory_space=pltpu.VMEM)
    return pl.pallas_call(
        finish_kernel,
        out_shape=(jax.ShapeDtypeStruct((own, block), bf16), jax.ShapeDtypeStruct((cols, rows), bf16)),
        in_specs=[vmem] * 5,
        out_specs=(vmem, vmem),
        scratch_shapes=[
            pltpu.VMEM((block, block), f32),
            pltpu.VMEM((block, block), f32),
            pltpu.VMEM((block, 128 + padded), f32),
            pltpu.VMEM((block, 128), f32),
            pltpu.VMEM((2 * block, rows), bf16),
            pltpu.VMEM((block, rows), f32),
        ],
        compiler_params=pltpu.CompilerParams(vmem_limit_bytes=48 << 20),
        name="finish",
    )(weights, mask, top, target, rest)


def per_device(calib, block_weight, rest_weight, prune_mask):
    block = prune_mask.shape[1]
    nd, nl = lax.axis_size("dp"), lax.axis_size("label")
    own = prune_mask.shape[0]
    label = lax.axis_index("label")
    width = calib.shape[1]
    rest_cols = rest_weight.shape[1]
    top, near, weights, mask = conjugate_gradients(
        calib,
        block_weight.T,
        prune_mask,
        block,
        rest_cols,
        calib.shape[0] * nd * nl,
        nd,
        nl,
    )
    weights = weights.reshape(block, -1)
    begin = window_start(label, block, rest_cols, near.shape[1], width)
    owned = lax.dynamic_slice_in_dim(near, block + label * rest_cols - begin, rest_cols, 1)
    pruned_block, updated_rest = finish(weights, mask, top, owned, rest_weight.T, own)
    return (pruned_block, updated_rest.T)


def solution(mesh):
    return jax.shard_map(
        per_device,
        mesh=mesh,
        in_specs=(
            P(("dp", "label"), None),
            P("dp", "label"),
            P("dp", "label"),
            P(("dp", "label"), None),
        ),
        out_specs=(P(("dp", "label"), None), P("dp", "label")),
        check_vma=False,
    )
```

```python
import functools
import math

import jax
import jax.numpy as jnp
from jax import lax
from jax.experimental import pallas as pl
from jax.experimental.pallas import tpu as pltpu
from jax.sharding import PartitionSpec as P

ITERS = 6
MESH = pl.DeviceIdType.MESH

damp_fraction = 0.01
sub_width = 16
CHUNKS = 7
FLIGHT = 4
LAG = 8
MEMBERS = 8


def two_terms(x):
    high = x.astype(jnp.bfloat16)
    low = (x - high.astype(jnp.float32)).astype(jnp.bfloat16)
    return jnp.concatenate([high, low], axis=0)


def loop(low, high, body):
    def step(d, carry):
        body(d)
        return carry

    lax.fori_loop(low, high, step, 0)


def remote(src, dst, send, recv, to):
    return pltpu.make_async_remote_copy(
        src_ref=src, dst_ref=dst, send_sem=send, recv_sem=recv, device_id=to, device_id_type=MESH
    )


def window_start(label, block, cols, window, width):
    return jnp.minimum((block + label * cols) // 128, (width - window) // 128) * 128


def window_width(block, cols, nl):
    return max(-(-((block + at * cols) % 128 + cols) // 128) * 128 for at in range(nl))


def place(nd, nl):
    nx = math.isqrt(nl // 2)
    ny, nz = nd // 2, nl // nx
    groups = (nx // 2) * (ny // 2) * (nz // 2)
    dp = lax.axis_index("dp")
    label = lax.axis_index("label")
    core, y, z, x = lax.rem(dp, 2), dp // 2, label // nx, lax.rem(label, nx)
    mx, my, mz = lax.rem(x, 2), lax.rem(y, 2), lax.rem(z, 2)
    qx, qy, qz = x // 2, y // 2, z // 2
    group = (qz * (ny // 2) + qy) * (nx // 2) + qx

    def member(e):
        hx, hy, hz = lax.rem(mx + lax.rem(e, 2), 2), lax.rem(my + lax.rem(e // 2, 2), 2), lax.rem(mz + e // 4, 2)
        return ((qy * 2 + hy) * 2 + core, (qz * 2 + hz) * nx + qx * 2 + hx), hz * 4 + hy * 2 + hx

    def other(h):
        q = lax.rem(group + h, groups)
        hx, hy, hz = lax.rem(q, nx // 2), lax.rem(q // (nx // 2), ny // 2), q // ((nx // 2) * (ny // 2))
        return ((hy * 2 + my) * 2 + core, (hz * 2 + mz) * nx + hx * 2 + mx)

    sets = (nx // 2) * (nz // 2)
    here = qz * (nx // 2) + qx

    def twin(h):
        q = lax.rem(here + h, sets)
        return (q // (nx // 2) * 2 + mz) * nx + lax.rem(q, nx // 2) * 2 + mx

    def fellow(j):
        return (qz * 2 + lax.rem(mz + j // 2, 2)) * nx + qx * 2 + lax.rem(mx + lax.rem(j, 2), 2)

    partner = (dp + 1 - 2 * core, label)
    return core, mz * 4 + my * 2 + mx, group, groups, member, other, partner, sets, twin, fellow


def cg_kernel(
    nd, nl, cols, tokens, calib_ref, w_ref, m_ref, top_ref, win_ref, wg_ref, mg_ref,
    c_ref, mask_ref, x_ref, pbuf, sbuf, rbuf, stbuf, vb, ab, img, xs, rs, ds, inv, damp_ref, diag_ref, rho_ref,
    cz, inner, stat, gs, gb, local_ref, part, slots,
    pair_s, pair_r, rs_s, rs_r, st_s, st_r, ag_s, ag_r, fw_s, fw_r, ab_s, ab_r, abf_s, abf_r,
    sp_s, sp_r, sm_s, sm_r, sg_s, sg_r, g_s, g_r, gf_s, gf_r, e_s, e_r, en_s, en_r, wt_s, wt_r, mt_s, mt_r, wf_s, wf_r, mf_s, mf_r, load,
):
    block = top_ref.shape[0]
    width = c_ref.shape[1]
    window = win_ref.shape[1]
    chunk = width // CHUNKS
    half = block // 2
    peers = MEMBERS - 1
    stat_rows = width // 128
    steps = ITERS - 1
    f32 = jnp.float32
    scale = 2.0 / tokens
    core, me, group, groups, member, other, partner, sets, twin, fellow = place(nd, nl)
    dp = lax.axis_index("dp")
    label = lax.axis_index("label")
    n = (nd // 2) * nl
    chip = (dp // 2) * nl + label
    own = m_ref.shape[0]

    def lanes(c):
        return pl.ds(c * chunk, chunk)

    def rows8(core_, g):
        return pl.ds(pl.multiple_of(core_ * half + g * 8, 8), 8)

    def rows16(core_, g):
        return pl.ds(pl.multiple_of(core_ * 2 * half + g * 16, 16), 16)

    half_rows = pl.ds(pl.multiple_of(core * half, half), half)
    away_rows = pl.ds(pl.multiple_of((1 - core) * half, half), half)
    half_rows16 = pl.ds(pl.multiple_of(core * 2 * half, 2 * half), 2 * half)
    mine = rows8(core, me)

    def chip_device(d):
        j = lax.rem(chip + d, n)
        return (2 * (j // nl) + core, lax.rem(j, nl))

    def columns(at):
        return (slice(None), pl.ds(pl.multiple_of(at * own, 128), own))

    def to_twin(h):
        to = (dp, twin(h))
        return (
            remote(wg_ref.at[label], wg_ref.at[label], wt_s.at[h], wt_r.at[h], to),
            remote(mg_ref.at[columns(label)], mg_ref.at[columns(label)], mt_s.at[h], mt_r.at[h], to),
        )

    half_lanes = wg_ref.shape[2] // 2
    half_block = block // 2

    def to_fellow(t, j):
        at = twin(sets - t // 2)
        to = (dp, fellow(j))
        w_part = wg_ref.at[at, :, pl.ds(pl.multiple_of(lax.rem(t, 2) * half_lanes, 128), half_lanes)]
        m_part = mg_ref.at[
            pl.ds(pl.multiple_of(lax.rem(t, 2) * half_block, 16), half_block),
            pl.ds(pl.multiple_of(at * own, 128), own),
        ]
        return (
            remote(w_part, w_part, wf_s.at[t], wf_r.at[t], to),
            remote(m_part, m_part, mf_s.at[t], mf_r.at[t], to),
        )

    def from_fellows(t):
        return (
            total_wait(wg_ref.at[pl.ds(0, 3), :, pl.ds(0, half_lanes)], wf_s.at[t], wf_r.at[t]),
            total_wait(mg_ref.at[pl.ds(0, half_block), pl.ds(0, 3 * own)], mf_s.at[t], mf_r.at[t]),
        )

    def tell_fellows(t):
        loop(1, 4, lambda j: [copy.start() for copy in to_fellow(t, j)])

    def pair(c):
        return remote(x_ref.at[c, away_rows], pbuf.at[c], pair_s.at[c], pair_r.at[c], partner)

    def forward(c):
        ref = vb.at[c, half_rows16]
        return remote(ref, ref, fw_s.at[c], fw_r.at[c], partner)

    def forward_ab():
        ref = ab.at[half_rows]
        return remote(ref, ref, abf_s, abf_r, partner)

    def total_wait(ref, send, recv):
        return remote(ref, ref, send, recv, partner)

    barrier = pltpu.get_barrier_semaphore()
    pl.semaphore_signal(barrier, inc=1, device_id=partner, device_id_type=MESH)
    loop(1, n, lambda d: pl.semaphore_signal(barrier, inc=1, device_id=chip_device(d), device_id_type=MESH))

    def product(lhs, terms, c):
        out = jnp.dot(lhs, c_ref[:, lanes(c)], preferred_element_type=f32)
        x_ref[c] = out[:block] + out[block:] if terms == 2 else out

    def scatter(c):
        pair(c).wait_recv()

        def send(d):
            e = MEMBERS - 1 - d
            to, g = member(e)
            sbuf[c, e] = x_ref[c, rows8(core, g)] + pbuf[c, pl.ds(pl.multiple_of(g * 8, 8), 8)]
            remote(sbuf.at[c, e], rbuf.at[c, e], rs_s.at[c], rs_r.at[c], to).start()

        loop(0, peers, send)

    def cross(c, par):
        acc = x_ref[c, mine] + pbuf[c, pl.ds(pl.multiple_of(me * 8, 8), 8)]
        total_wait(rbuf.at[c, pl.ds(1, peers)], rs_s.at[c], rs_r.at[c]).wait_recv()
        for e in range(1, MEMBERS):
            acc = acc + rbuf[c, e]
        stbuf[par, c, group] = acc
        ref = stbuf.at[par, c, group]
        loop(1, groups, lambda h: remote(ref, ref, st_s.at[par, c], st_r.at[par, c], other(h)).start())

    def total_image(c, par, first):
        if groups > 1:
            total_wait(stbuf.at[par, c, pl.ds(0, groups - 1)], st_s.at[par, c], st_r.at[par, c]).wait_recv()
        acc = stbuf[par, c, 0]
        for h in range(1, groups):
            acc = acc + stbuf[par, c, h]
        if first:
            acc = acc / diag_ref[...]
        direction = ds[:, lanes(c)]
        image = scale * acc + damp_ref[0:8, 0:1] * direction
        img[:, lanes(c)] = image
        return image * inv[:, lanes(c)], jnp.sum(direction * image, axis=1, keepdims=True)

    def publish(slot, terms):
        vb[slot, rows16(core, me)] = terms

        def send(d):
            to, g = member(MEMBERS - 1 - d)
            ref = vb.at[slot, rows16(core, me)]
            remote(ref, ref, ag_s.at[slot], ag_r.at[slot], to).start()

        loop(0, peers, send)

    def publisher(par, first, last):
        curves = []
        held = []

        def step(c):
            term, part_curve = total_image(c, par, first)
            curves.append(part_curve)
            if not last:
                publish(c, two_terms(term))
                return
            held.append(term)
            if c + 1 == CHUNKS and len(held) == 1:
                held.append(jnp.zeros_like(term))
            if len(held) == 2:
                publish(c // 2, jnp.concatenate(held, axis=0).astype(jnp.bfloat16))
                held.clear()

        return step, curves

    def rescale(curve):
        rho = rho_ref[:, 0:1]
        alpha = rho / curve
        fresh = jnp.zeros((8, 1), f32)
        for c in range(CHUNKS):
            resid = rs[:, lanes(c)] - alpha * img[:, lanes(c)]
            rs[:, lanes(c)] = resid
            fresh = fresh + jnp.sum(resid * resid * inv[:, lanes(c)], axis=1, keepdims=True)
        beta = fresh / rho
        lane = lax.broadcasted_iota(jnp.int32, (8, 128), 1)
        ab[mine] = jnp.where(lane < 64, alpha, beta)

        def send(d):
            to, g = member(MEMBERS - 1 - d)
            remote(ab.at[mine], ab.at[mine], ab_s, ab_r, to).start()

        loop(0, peers, send)
        rho_ref[...] = jnp.broadcast_to(fresh, (8, 128))
        for c in range(CHUNKS):
            direction = ds[:, lanes(c)]
            xs[:, lanes(c)] = xs[:, lanes(c)] + alpha * direction
            ds[:, lanes(c)] = rs[:, lanes(c)] * inv[:, lanes(c)] + beta * direction

    def gather(c):
        total_wait(vb.at[c, pl.ds(0, peers * 16)], ag_s.at[c], ag_r.at[c]).wait_recv()
        forward(c).start()

    def times_calib(slot, c):
        return lax.dot_general(
            vb[slot], c_ref[:, lanes(c)], (((1,), (1,)), ((), ())), preferred_element_type=f32
        )

    def applied(slots, last):
        one_term, other_term = None, None
        for slot in range(slots):
            forward(slot).wait_recv()
            if not last:
                out = times_calib(slot, slot)
                one_term = out if one_term is None else one_term + out
            else:
                out = times_calib(slot, 2 * slot)
                one_term = out if one_term is None else one_term + out
                if 2 * slot + 1 < CHUNKS:
                    out = times_calib(slot, 2 * slot + 1)
                    other_term = out if other_term is None else other_term + out
        if other_term is None:
            other_term = one_term
        one_term = one_term.reshape(2 * block // 16, 2, 8, one_term.shape[1])
        other_term = other_term.reshape(one_term.shape)
        return (one_term[:, 0] + other_term[:, 1]).reshape(block, one_term.shape[3])

    def finish_sends(slots=CHUNKS):
        for c in range(slots):
            total_wait(vb.at[c, pl.ds(0, peers * 16)], ag_s.at[c], ag_r.at[c]).wait_send()
            forward(c).wait_send()
        total_wait(ab.at[pl.ds(0, peers * 8)], ab_s, ab_r).wait_send()
        forward_ab().wait_send()

    def message(at):
        return pl.ds(pl.multiple_of(window_start(at, block, cols, window, width), 128), window)

    def fill(ref, at, where, facts):
        view = message(at)
        ref[where + (slice(0, 128),)] = xs[:, 0:128]
        ref[where + (slice(128, 128 + window),)] = xs[:, view]
        ref[where + (slice(128 + window, 256 + window),)] = ds[:, 0:128]
        ref[where + (slice(256 + window, 256 + 2 * window),)] = ds[:, view]
        ref[where + (slice(256 + 2 * window, 384 + 2 * window),)] = facts

    def tell_all():
        lane8 = lax.broadcasted_iota(jnp.int32, (8, 128), 1)
        power = jnp.sum(ds[...] * ds[...], axis=1, keepdims=True)
        facts = jnp.where(lane8 < 64, rho_ref[...], power)

        def tell(d):
            e = MEMBERS - 1 - d
            to, g = member(e)
            fill(gs, to[1], (e, slice(None)), facts)
            remote(gs.at[e], gb.at[mine], g_s, g_r, to).start()

        loop(0, peers, tell)
        fill(gb, label, (mine,), facts)

    def reduce_and_apply(par, first, last, index):
        publish_chunk, curves = publisher(par, first, last)
        for t in range(CHUNKS + LAG):
            if t < CHUNKS:
                scatter(t)
                if first and t == 0:
                    share_stats()
            c = t - FLIGHT
            if 0 <= c < CHUNKS:
                cross(c, par)
                if first and c == 0:
                    cross_stats()
                if first and c + 1 == CHUNKS:
                    loop(1, sets, lambda h: [copy.start() for copy in to_twin(h)])
            c = t - LAG
            if 0 <= c < CHUNKS:
                if first and c == 0:
                    start_state()
                publish_chunk(c)
        rescale(sum(curves[1:], curves[0]))
        for c in range(CHUNKS):
            pair(c).wait_send()
            total_wait(sbuf.at[c, pl.ds(1, peers)], rs_s.at[c], rs_r.at[c]).wait_send()
        if last:
            tell_all()
        slots = -(-CHUNKS // 2) if last else CHUNKS
        for slot in range(slots):
            gather(slot)
        total_wait(ab.at[pl.ds(0, peers * 8)], ab_s, ab_r).wait_recv()
        forward_ab().start()
        if not first:
            begin = (index - 1) * share
            loop(begin, jnp.minimum(begin + share, 2 * sets), tell_fellows)
        if groups > 1:
            for c in range(CHUNKS):
                total_wait(stbuf.at[par, c, pl.ds(0, groups - 1)], st_s.at[par, c], st_r.at[par, c]).wait_send()
        out = applied(slots, last)
        forward_ab().wait_recv()
        applied_z = cz[...] - ab[:, 0:1] * out
        cz[...] = applied_z
        inner[...] = applied_z + ab[:, 64:65] * inner[...]

    def begin_step(lhs, terms):
        for c in range(CHUNKS):
            product(lhs, terms, c)
            pair(c).start()

    local_stat, near_stat, member_stat, group_stat = 0, 1, 2, 2 + MEMBERS

    def pair_stats():
        return remote(stat.at[local_stat], stat.at[near_stat], sp_s, sp_r, partner)

    def share_stats():
        pair_stats().wait_recv()
        stat[member_stat + me] = stat[local_stat] + stat[near_stat]
        ref = stat.at[member_stat + me]
        loop(1, MEMBERS, lambda e: remote(ref, ref, sm_s, sm_r, member(e)[0]).start())

    def cross_stats():
        total_wait(stat.at[pl.ds(member_stat, peers)], sm_s, sm_r).wait_recv()
        acc = stat[member_stat]
        for e in range(1, MEMBERS):
            acc = acc + stat[member_stat + e]
        stat[group_stat + group] = acc
        ref = stat.at[group_stat + group]
        loop(1, groups, lambda h: remote(ref, ref, sg_s, sg_r, other(h)).start())

    def start_state():
        if groups > 1:
            total_wait(stat.at[pl.ds(group_stat, groups - 1)], sg_s, sg_r).wait_recv()
        acc = stat[group_stat]
        for h in range(1, groups):
            acc = acc + stat[group_stat + h]
        damping = damp_fraction * 2.0 * jnp.sum(
            jnp.sum(acc, axis=0, keepdims=True), axis=1, keepdims=True
        ) / (tokens * width)
        damp_ref[...] = jnp.broadcast_to(damping, damp_ref.shape)
        diag = scale * acc + damping
        inverse = 1.0 / diag
        for j in range(stat_rows):
            inv[:, j * 128 : (j + 1) * 128] = jnp.broadcast_to(inverse[j : j + 1, :], (8, 128))
        row = lax.broadcasted_iota(jnp.int32, (block, 128), 0)
        lane = lax.broadcasted_iota(jnp.int32, (block, 128), 1)
        every = jnp.sum(jnp.where(row == lane, diag[0:1, :], 0.0), axis=1, keepdims=True)
        row8 = lax.broadcasted_iota(jnp.int32, (8, 128), 0) + core * half + me * 8
        lane8 = lax.broadcasted_iota(jnp.int32, (8, 128), 1)
        unit = jnp.where(row8 == lane8, 1.0, 0.0)
        own_diag = jnp.sum(unit * diag[0:1, :], axis=1, keepdims=True)
        diag_ref[...] = own_diag
        rho_ref[...] = jnp.broadcast_to(1.0 / own_diag, (8, 128))
        rs[...] = jnp.zeros_like(rs)
        ds[...] = jnp.zeros_like(ds)
        xs[...] = jnp.zeros_like(xs)
        rs[:, 0:128] = unit
        ds[:, 0:128] = unit / own_diag
        scaled = cz[...] / every
        cz[...] = scaled
        inner[...] = scaled
        pair_stats().wait_send()
        total_wait(stat.at[pl.ds(member_stat, peers)], sm_s, sm_r).wait_send()
        if groups > 1:
            total_wait(stat.at[pl.ds(group_stat, groups - 1)], sg_s, sg_r).wait_send()

    share = -(-2 * sets // (steps - 1))

    def fetch(c):
        return pltpu.make_async_copy(calib_ref.at[:, lanes(c)], c_ref.at[:, lanes(c)], load.at[c])

    for c in range(CHUNKS):
        fetch(c).start()
    fetch_mask = pltpu.make_async_copy(m_ref, mask_ref, load.at[CHUNKS])
    fetch_weights = pltpu.make_async_copy(w_ref, wg_ref.at[label], load.at[CHUNKS + 1])
    fetch_mask.start()
    fetch_weights.start()
    one = jnp.where(
        lax.broadcasted_iota(jnp.int32, (block, 128), 0) == lax.broadcasted_iota(jnp.int32, (block, 128), 1), 1.0, 0.0
    )
    fetch(0).wait()
    turned = lax.dot_general(
        one.astype(jnp.bfloat16), c_ref[:, 0:block], (((1,), (1,)), ((), ())), preferred_element_type=f32
    )
    cz[...] = turned
    lhs = turned.astype(jnp.bfloat16)
    product(lhs, 1, 0)
    stat[local_stat] = jnp.zeros(stat.shape[1:], f32)
    for c in range(CHUNKS):
        if c:
            fetch(c).wait()
        for j in range(c * chunk // 128, (c + 1) * chunk // 128):
            square = c_ref[:, j * 128 : (j + 1) * 128].astype(f32)
            stat[local_stat, j : j + 1, :] = jnp.sum(square * square, axis=0, keepdims=True)
    pl.semaphore_wait(barrier, n)
    pair_stats().start()
    pair(0).start()
    for c in range(1, CHUNKS):
        product(lhs, 1, c)
        pair(c).start()
    fetch_mask.wait()
    mg_ref[columns(label)] = mask_ref[...].astype(f32).T.astype(jnp.bfloat16)
    fetch_weights.wait()
    reduce_and_apply(0, True, False, 0)
    loop(1, sets, lambda h: [copy.wait_recv() for copy in to_twin(h)])

    def iteration(index, carry):
        begin_step(two_terms(inner[...]), 2)
        finish_sends()
        reduce_and_apply(lax.rem(index, 2), False, False, index)
        return carry

    lax.fori_loop(1, steps - 1, iteration, 0)
    begin_step(two_terms(inner[...]), 2)
    finish_sends()
    reduce_and_apply((steps - 1) % 2, False, True, steps - 1)
    energy = inner[...]
    local_ref[...] = lax.dot_general(
        jnp.ones((8, energy.shape[1]), f32),
        energy * energy,
        (((1,), (1,)), ((), ())),
        precision=lax.Precision.HIGHEST,
        preferred_element_type=f32,
    )
    near = remote(local_ref, part, e_s, e_r, partner)
    near.start()
    near.wait_recv()
    slots[chip] = local_ref[...] + part[...]

    def far(d, j):
        return remote(slots.at[j], slots.at[j], en_s, en_r, chip_device(d))

    loop(1, n, lambda d: far(d, chip).start())
    finish_sends(-(-CHUNKS // 2))
    loop(1, sets, lambda h: [copy.wait_send() for copy in to_twin(h)])
    loop(0, 2 * sets, lambda t: [copy.wait_send() for copy in from_fellows(t)])
    loop(0, 2 * sets, lambda t: [copy.wait_recv() for copy in from_fellows(t)])
    total_wait(slots.at[pl.ds(0, n - 1)], en_s, en_r).wait_recv()
    norms = lax.fori_loop(1, n, lambda j, acc: acc + slots[j], slots[0])
    total_wait(gb.at[pl.ds(0, peers * 8)], g_s, g_r).wait_recv()
    last = remote(gb.at[half_rows], gb.at[half_rows], gf_s, gf_r, partner)
    last.start()
    near.wait_send()
    total_wait(slots.at[pl.ds(0, n - 1)], en_s, en_r).wait_send()
    total_wait(gs.at[pl.ds(1, peers)], g_s, g_r).wait_send()
    last.wait_recv()
    curve = scale * jnp.sum(one * norms[0:1, :], axis=1, keepdims=True)
    rho = gb[:, 256 + 2 * window : 257 + 2 * window]
    power = gb[:, 320 + 2 * window : 321 + 2 * window]
    alpha = rho / (curve + damp_ref[0:1, 0:1] * power)
    top_ref[...] = gb[:, 0:128] + alpha * gb[:, 128 + window : 256 + window]
    win_ref[...] = gb[:, 128 : 128 + window] + alpha * gb[:, 256 + window : 256 + 2 * window]
    last.wait_send()


def conjugate_gradients(calib, w, mask, block, cols, tokens, nd, nl):
    width = calib.shape[1]
    window = window_width(block, cols, nl)
    nx = math.isqrt(nl // 2)
    groups = (nx // 2) * (nd // 4) * (nl // nx // 2)
    sets = (nx // 2) * (nl // nx // 2)
    n = nd // 2 * nl
    chunk = width // CHUNKS
    f32, bf16 = jnp.float32, jnp.bfloat16
    vmem = pl.BlockSpec(memory_space=pltpu.VMEM)
    dma = pltpu.SemaphoreType.DMA
    stat_rows = -(-(width // 128) // 8) * 8
    message = 384 + 2 * window
    return pl.pallas_call(
        functools.partial(cg_kernel, nd, nl, cols, tokens),
        out_shape=(
            jax.ShapeDtypeStruct((block, 128), f32),
            jax.ShapeDtypeStruct((block, window), f32),
            jax.ShapeDtypeStruct((nl,) + w.shape, w.dtype),
            jax.ShapeDtypeStruct((block, mask.shape[0] * nl), bf16),
        ),
        in_specs=[pl.BlockSpec(memory_space=pltpu.HBM)] * 3,
        out_specs=(vmem,) * 4,
        scratch_shapes=[
            pltpu.VMEM(calib.shape, bf16),
            pltpu.VMEM(mask.shape, mask.dtype),
            pltpu.VMEM((CHUNKS, block, chunk), f32),
            pltpu.VMEM((CHUNKS, block // 2, chunk), f32),
            pltpu.VMEM((CHUNKS, MEMBERS, 8, chunk), f32),
            pltpu.VMEM((CHUNKS, MEMBERS, 8, chunk), f32),
            pltpu.VMEM((2, CHUNKS, groups, 8, chunk), f32),
            pltpu.VMEM((CHUNKS, 2 * block, chunk), bf16),
            pltpu.VMEM((block, 128), f32),
            pltpu.VMEM((8, width), f32),
            pltpu.VMEM((8, width), f32),
            pltpu.VMEM((8, width), f32),
            pltpu.VMEM((8, width), f32),
            pltpu.VMEM((8, width), f32),
            pltpu.VMEM((8, 128), f32),
            pltpu.VMEM((8, 1), f32),
            pltpu.VMEM((8, 128), f32),
            pltpu.VMEM((block, calib.shape[0]), f32),
            pltpu.VMEM((block, calib.shape[0]), f32),
            pltpu.VMEM((2 + MEMBERS + groups, stat_rows, 128), f32),
            pltpu.VMEM((MEMBERS, 8, message), f32),
            pltpu.VMEM((block, message), f32),
            pltpu.VMEM((8, block), f32),
            pltpu.VMEM((8, block), f32),
            pltpu.VMEM((n, 8, block), f32),
        ]
        + [dma((CHUNKS,))] * 4
        + [dma((2, CHUNKS))] * 2
        + [dma((CHUNKS,))] * 4
        + [dma] * 4
        + [dma] * 6
        + [dma] * 4
        + [dma] * 4
        + [dma((sets,))] * 4
        + [dma((2 * sets,))] * 4
        + [dma((CHUNKS + 2,))],
        compiler_params=pltpu.CompilerParams(collective_id=0, has_side_effects=True, vmem_limit_bytes=48 << 20),
        name="conjugate_gradients",
    )(calib, w, mask)


def finish_kernel(w_ref, m_ref, top_ref, t_ref, rest_ref, kept_ref, out_ref, sym, lower, tri, scales, errors, kept):
    block, rows = w_ref.shape
    own = kept_ref.shape[0]
    cols = rest_ref.shape[0]
    width = tri.shape[1]
    f32, bf16 = jnp.float32, jnp.bfloat16
    group = 512 if rows % 512 == 0 else rows
    top = top_ref[...]
    sym[...] = 0.5 * (top + top.T)
    lower[...] = jnp.zeros_like(lower)
    errors[...] = jnp.zeros_like(errors)
    tri[...] = jnp.zeros_like(tri)
    row = lax.broadcasted_iota(jnp.int32, (sub_width, 128), 0)

    def wide(x, lanes):
        return jnp.concatenate([x] * (lanes // 128), axis=1)

    def split(x):
        high = x.astype(bf16)
        return high, (x - high.astype(f32)).astype(bf16)

    for begin in range(0, block, sub_width):
        at = slice(begin, begin + sub_width)
        target = jnp.concatenate([sym[at, :], t_ref[at, :]], axis=1)
        if begin:
            factor = lower[...].T[at, :]
            target = target - jnp.dot(
                factor, tri[...], precision=lax.Precision.HIGHEST, preferred_element_type=f32
            )
            high, low = split(factor)
            factors = jnp.concatenate(
                [jnp.concatenate([high, high], axis=1), jnp.concatenate([low, jnp.zeros_like(low)], axis=1)], axis=0
            )
        spread = [
            jnp.broadcast_to(target[:, begin + j : begin + j + 1], (sub_width, 128)) for j in range(sub_width)
        ]
        steps = []
        inverses = []
        for j in range(sub_width):
            inverse = 1.0 / spread[j][j : j + 1, :]
            step = jnp.where(row > j, spread[j] * inverse, 0.0)
            for k in range(j + 1, sub_width):
                spread[k] = spread[k] - step * spread[k][j : j + 1, :]
            steps.append(step)
            inverses.append(inverse)
        for j in range(sub_width):
            target = target - wide(steps[j], width) * target[j : j + 1, :]
        tri[at, :] = target
        inverse = jnp.concatenate(inverses, axis=0)
        scales[at, :] = inverse
        lower[at, :] = target[:, :block] * inverse
        for first in range(0, rows, group):
            lanes = slice(first, first + group)
            window = w_ref[at, lanes].astype(f32)
            chosen = m_ref[at, lanes].astype(f32)
            if begin:
                both = jnp.dot(factors, errors[:, lanes], preferred_element_type=f32)
                window = window - (both[:sub_width] + both[sub_width:])
            for j in range(sub_width):
                window = window - wide(steps[j], group) * (chosen[j : j + 1, :] * window[j : j + 1, :])
            error = chosen * window
            high, low = split(error)
            errors[at, lanes] = high
            errors[slice(block + begin, block + begin + sub_width), lanes] = low
            kept[at, lanes] = window - error
    label = lax.axis_index("label")
    kept_ref[...] = kept[:, pl.ds(pl.multiple_of(label * own, 128), own)].T.astype(kept_ref.dtype)
    cross = (tri[:, 128:] * wide(scales[...], width - 128)).T[:cols]
    high, low = split(cross)
    twice = jnp.concatenate([high, high], axis=1)
    for first in range(0, rows, group):
        lanes = slice(first, first + group)
        delta = jnp.dot(twice, errors[:, lanes], preferred_element_type=f32)
        delta = delta + jnp.dot(low, errors[:block, lanes], preferred_element_type=f32)
        out_ref[:, lanes] = (rest_ref[:, lanes].astype(f32) - delta).astype(out_ref.dtype)


def finish(weights, mask, top, target, rest, own):
    block, rows = weights.shape
    cols = rest.shape[0]
    f32, bf16 = jnp.float32, jnp.bfloat16
    padded = -(-cols // 128) * 128
    target = jnp.pad(target, ((0, 0), (0, padded - cols)))
    vmem = pl.BlockSpec(memory_space=pltpu.VMEM)
    return pl.pallas_call(
        finish_kernel,
        out_shape=(jax.ShapeDtypeStruct((own, block), bf16), jax.ShapeDtypeStruct((cols, rows), bf16)),
        in_specs=[vmem] * 5,
        out_specs=(vmem, vmem),
        scratch_shapes=[
            pltpu.VMEM((block, block), f32),
            pltpu.VMEM((block, block), f32),
            pltpu.VMEM((block, 128 + padded), f32),
            pltpu.VMEM((block, 128), f32),
            pltpu.VMEM((2 * block, rows), bf16),
            pltpu.VMEM((block, rows), f32),
        ],
        compiler_params=pltpu.CompilerParams(vmem_limit_bytes=48 << 20),
        name="finish",
    )(weights, mask, top, target, rest)


def per_device(calib, block_weight, rest_weight, prune_mask):
    block = prune_mask.shape[1]
    nd, nl = lax.axis_size("dp"), lax.axis_size("label")
    own = prune_mask.shape[0]
    label = lax.axis_index("label")
    width = calib.shape[1]
    rest_cols = rest_weight.shape[1]
    top, near, weights, mask = conjugate_gradients(
        calib,
        block_weight.T,
        prune_mask,
        block,
        rest_cols,
        calib.shape[0] * nd * nl,
        nd,
        nl,
    )
    weights = weights.reshape(block, -1)
    begin = window_start(label, block, rest_cols, near.shape[1], width)
    owned = lax.dynamic_slice_in_dim(near, block + label * rest_cols - begin, rest_cols, 1)
    pruned_block, updated_rest = finish(weights, mask, top, owned, rest_weight.T, own)
    return (pruned_block, updated_rest.T)


def solution(mesh):
    return jax.shard_map(
        per_device,
        mesh=mesh,
        in_specs=(
            P(("dp", "label"), None),
            P("dp", "label"),
            P("dp", "label"),
            P(("dp", "label"), None),
        ),
        out_specs=(P(("dp", "label"), None), P("dp", "label")),
        check_vma=False,
    )
```

```python
import functools
import math

import jax
import jax.numpy as jnp
from jax import lax
from jax.experimental import pallas as pl
from jax.experimental.pallas import tpu as pltpu
from jax.sharding import PartitionSpec as P

ITERS = 6
MESH = pl.DeviceIdType.MESH

damp_fraction = 0.01
sub_width = 16
CHUNKS = 7
FLIGHT = 4
LAG = 8
MEMBERS = 8


def two_terms(x):
    high = x.astype(jnp.bfloat16)
    low = (x - high.astype(jnp.float32)).astype(jnp.bfloat16)
    return jnp.concatenate([high, low], axis=0)


def loop(low, high, body):
    def step(d, carry):
        body(d)
        return carry

    lax.fori_loop(low, high, step, 0)


def remote(src, dst, send, recv, to):
    return pltpu.make_async_remote_copy(
        src_ref=src, dst_ref=dst, send_sem=send, recv_sem=recv, device_id=to, device_id_type=MESH
    )


def window_start(label, block, cols, window, width):
    return jnp.minimum((block + label * cols) // 128, (width - window) // 128) * 128


def window_width(block, cols, nl):
    return max(-(-((block + at * cols) % 128 + cols) // 128) * 128 for at in range(nl))


def place(nd, nl):
    nx = math.isqrt(nl // 2)
    ny, nz = nd // 2, nl // nx
    groups = (nx // 2) * (ny // 2) * (nz // 2)
    dp = lax.axis_index("dp")
    label = lax.axis_index("label")
    core, y, z, x = lax.rem(dp, 2), dp // 2, label // nx, lax.rem(label, nx)
    mx, my, mz = lax.rem(x, 2), lax.rem(y, 2), lax.rem(z, 2)
    qx, qy, qz = x // 2, y // 2, z // 2
    group = (qz * (ny // 2) + qy) * (nx // 2) + qx

    def member(e):
        hx, hy, hz = lax.rem(mx + lax.rem(e, 2), 2), lax.rem(my + lax.rem(e // 2, 2), 2), lax.rem(mz + e // 4, 2)
        return ((qy * 2 + hy) * 2 + core, (qz * 2 + hz) * nx + qx * 2 + hx), hz * 4 + hy * 2 + hx

    def other(h):
        q = lax.rem(group + h, groups)
        hx, hy, hz = lax.rem(q, nx // 2), lax.rem(q // (nx // 2), ny // 2), q // ((nx // 2) * (ny // 2))
        return ((hy * 2 + my) * 2 + core, (hz * 2 + mz) * nx + hx * 2 + mx)

    sets = (nx // 2) * (nz // 2)
    here = qz * (nx // 2) + qx

    def twin(h):
        q = lax.rem(here + h, sets)
        return (q // (nx // 2) * 2 + mz) * nx + lax.rem(q, nx // 2) * 2 + mx

    def fellow(j):
        return (qz * 2 + lax.rem(mz + j // 2, 2)) * nx + qx * 2 + lax.rem(mx + lax.rem(j, 2), 2)

    partner = (dp + 1 - 2 * core, label)
    return core, mz * 4 + my * 2 + mx, group, groups, member, other, partner, sets, twin, fellow


def cg_kernel(
    nd, nl, cols, tokens, calib_ref, w_ref, m_ref, top_ref, win_ref, wg_ref, mg_ref,
    c_ref, mask_ref, x_ref, pbuf, sbuf, rbuf, stbuf, vb, ab, img, xs, rs, ds, inv, damp_ref, diag_ref, rho_ref,
    cz, inner, stat, gs, gb, local_ref, part, slots,
    pair_s, pair_r, rs_s, rs_r, st_s, st_r, ag_s, ag_r, fw_s, fw_r, ab_s, ab_r, abf_s, abf_r,
    sp_s, sp_r, sm_s, sm_r, sg_s, sg_r, g_s, g_r, gf_s, gf_r, e_s, e_r, en_s, en_r, wt_s, wt_r, mt_s, mt_r, wf_s, wf_r, mf_s, mf_r, load,
):
    block = top_ref.shape[0]
    width = c_ref.shape[1]
    window = win_ref.shape[1]
    chunk = width // CHUNKS
    half = block // 2
    peers = MEMBERS - 1
    stat_rows = width // 128
    steps = ITERS - 1
    f32 = jnp.float32
    scale = 2.0 / tokens
    core, me, group, groups, member, other, partner, sets, twin, fellow = place(nd, nl)
    dp = lax.axis_index("dp")
    label = lax.axis_index("label")
    n = (nd // 2) * nl
    chip = (dp // 2) * nl + label
    own = m_ref.shape[0]

    def lanes(c):
        return pl.ds(c * chunk, chunk)

    def rows8(core_, g):
        return pl.ds(pl.multiple_of(core_ * half + g * 8, 8), 8)

    def rows16(core_, g):
        return pl.ds(pl.multiple_of(core_ * 2 * half + g * 16, 16), 16)

    half_rows = pl.ds(pl.multiple_of(core * half, half), half)
    away_rows = pl.ds(pl.multiple_of((1 - core) * half, half), half)
    half_rows16 = pl.ds(pl.multiple_of(core * 2 * half, 2 * half), 2 * half)
    mine = rows8(core, me)

    def chip_device(d):
        j = lax.rem(chip + d, n)
        return (2 * (j // nl) + core, lax.rem(j, nl))

    def columns(at):
        return (slice(None), pl.ds(pl.multiple_of(at * own, 128), own))

    def to_twin(h):
        to = (dp, twin(h))
        return (
            remote(wg_ref.at[label], wg_ref.at[label], wt_s.at[h], wt_r.at[h], to),
            remote(mg_ref.at[columns(label)], mg_ref.at[columns(label)], mt_s.at[h], mt_r.at[h], to),
        )

    half_lanes = wg_ref.shape[2] // 2
    half_block = block // 2

    def to_fellow(t, j):
        at = twin(sets - t // 2)
        to = (dp, fellow(j))
        w_part = wg_ref.at[at, :, pl.ds(pl.multiple_of(lax.rem(t, 2) * half_lanes, 128), half_lanes)]
        m_part = mg_ref.at[
            pl.ds(pl.multiple_of(lax.rem(t, 2) * half_block, 16), half_block),
            pl.ds(pl.multiple_of(at * own, 128), own),
        ]
        return (
            remote(w_part, w_part, wf_s.at[t], wf_r.at[t], to),
            remote(m_part, m_part, mf_s.at[t], mf_r.at[t], to),
        )

    def from_fellows(t):
        return (
            total_wait(wg_ref.at[pl.ds(0, 3), :, pl.ds(0, half_lanes)], wf_s.at[t], wf_r.at[t]),
            total_wait(mg_ref.at[pl.ds(0, half_block), pl.ds(0, 3 * own)], mf_s.at[t], mf_r.at[t]),
        )

    def tell_fellows(t):
        loop(1, 4, lambda j: [copy.start() for copy in to_fellow(t, j)])

    def pair(c):
        return remote(x_ref.at[c, away_rows], pbuf.at[c], pair_s.at[c], pair_r.at[c], partner)

    def forward(c):
        ref = vb.at[c, half_rows16]
        return remote(ref, ref, fw_s.at[c], fw_r.at[c], partner)

    def forward_ab():
        ref = ab.at[half_rows]
        return remote(ref, ref, abf_s, abf_r, partner)

    def total_wait(ref, send, recv):
        return remote(ref, ref, send, recv, partner)

    barrier = pltpu.get_barrier_semaphore()
    pl.semaphore_signal(barrier, inc=1, device_id=partner, device_id_type=MESH)
    loop(1, n, lambda d: pl.semaphore_signal(barrier, inc=1, device_id=chip_device(d), device_id_type=MESH))

    def product(lhs, terms, c):
        out = jnp.dot(lhs, c_ref[:, lanes(c)], preferred_element_type=f32)
        x_ref[c] = out[:block] + out[block:] if terms == 2 else out

    def scatter(c):
        pair(c).wait_recv()

        def send(d):
            e = MEMBERS - 1 - d
            to, g = member(e)
            sbuf[c, e] = x_ref[c, rows8(core, g)] + pbuf[c, pl.ds(pl.multiple_of(g * 8, 8), 8)]
            remote(sbuf.at[c, e], rbuf.at[c, e], rs_s.at[c], rs_r.at[c], to).start()

        loop(0, peers, send)

    def cross(c, par):
        acc = x_ref[c, mine] + pbuf[c, pl.ds(pl.multiple_of(me * 8, 8), 8)]
        total_wait(rbuf.at[c, pl.ds(1, peers)], rs_s.at[c], rs_r.at[c]).wait_recv()
        for e in range(1, MEMBERS):
            acc = acc + rbuf[c, e]
        stbuf[par, c, group] = acc
        ref = stbuf.at[par, c, group]
        loop(1, groups, lambda h: remote(ref, ref, st_s.at[par, c], st_r.at[par, c], other(h)).start())

    def total_image(c, par, first):
        if groups > 1:
            total_wait(stbuf.at[par, c, pl.ds(0, groups - 1)], st_s.at[par, c], st_r.at[par, c]).wait_recv()
        acc = stbuf[par, c, 0]
        for h in range(1, groups):
            acc = acc + stbuf[par, c, h]
        if first:
            acc = acc / diag_ref[...]
        direction = ds[:, lanes(c)]
        image = scale * acc + damp_ref[0:8, 0:1] * direction
        img[:, lanes(c)] = image
        return image * inv[:, lanes(c)], jnp.sum(direction * image, axis=1, keepdims=True)

    def publish(slot, terms):
        vb[slot, rows16(core, me)] = terms

        def send(d):
            to, g = member(MEMBERS - 1 - d)
            ref = vb.at[slot, rows16(core, me)]
            remote(ref, ref, ag_s.at[slot], ag_r.at[slot], to).start()

        loop(0, peers, send)

    def publisher(par, first, last):
        curves = []
        held = []

        def step(c):
            term, part_curve = total_image(c, par, first)
            curves.append(part_curve)
            if not last:
                publish(c, two_terms(term))
                return
            held.append(term)
            if c + 1 == CHUNKS and len(held) == 1:
                held.append(jnp.zeros_like(term))
            if len(held) == 2:
                publish(c // 2, jnp.concatenate(held, axis=0).astype(jnp.bfloat16))
                held.clear()

        return step, curves

    def rescale(curve):
        rho = rho_ref[:, 0:1]
        alpha = rho / curve
        fresh = jnp.zeros((8, 1), f32)
        for c in range(CHUNKS):
            resid = rs[:, lanes(c)] - alpha * img[:, lanes(c)]
            rs[:, lanes(c)] = resid
            fresh = fresh + jnp.sum(resid * resid * inv[:, lanes(c)], axis=1, keepdims=True)
        beta = fresh / rho
        lane = lax.broadcasted_iota(jnp.int32, (8, 128), 1)
        ab[mine] = jnp.where(lane < 64, alpha, beta)

        def send(d):
            to, g = member(MEMBERS - 1 - d)
            remote(ab.at[mine], ab.at[mine], ab_s, ab_r, to).start()

        loop(0, peers, send)
        rho_ref[...] = jnp.broadcast_to(fresh, (8, 128))
        for c in range(CHUNKS):
            direction = ds[:, lanes(c)]
            xs[:, lanes(c)] = xs[:, lanes(c)] + alpha * direction
            ds[:, lanes(c)] = rs[:, lanes(c)] * inv[:, lanes(c)] + beta * direction

    def gather(c):
        total_wait(vb.at[c, pl.ds(0, peers * 16)], ag_s.at[c], ag_r.at[c]).wait_recv()
        forward(c).start()

    def times_calib(slot, c):
        return lax.dot_general(
            vb[slot], c_ref[:, lanes(c)], (((1,), (1,)), ((), ())), preferred_element_type=f32
        )

    def applied(slots, last):
        one_term, other_term = None, None
        for slot in range(slots):
            forward(slot).wait_recv()
            if not last:
                out = times_calib(slot, slot)
                one_term = out if one_term is None else one_term + out
            else:
                out = times_calib(slot, 2 * slot)
                one_term = out if one_term is None else one_term + out
                if 2 * slot + 1 < CHUNKS:
                    out = times_calib(slot, 2 * slot + 1)
                    other_term = out if other_term is None else other_term + out
        if other_term is None:
            other_term = one_term
        one_term = one_term.reshape(2 * block // 16, 2, 8, one_term.shape[1])
        other_term = other_term.reshape(one_term.shape)
        return (one_term[:, 0] + other_term[:, 1]).reshape(block, one_term.shape[3])

    def finish_sends(slots=CHUNKS):
        for c in range(slots):
            total_wait(vb.at[c, pl.ds(0, peers * 16)], ag_s.at[c], ag_r.at[c]).wait_send()
            forward(c).wait_send()
        total_wait(ab.at[pl.ds(0, peers * 8)], ab_s, ab_r).wait_send()
        forward_ab().wait_send()

    def message(at):
        return pl.ds(pl.multiple_of(window_start(at, block, cols, window, width), 128), window)

    def fill(ref, at, where, facts):
        view = message(at)
        ref[where + (slice(0, 128),)] = xs[:, 0:128]
        ref[where + (slice(128, 128 + window),)] = xs[:, view]
        ref[where + (slice(128 + window, 256 + window),)] = ds[:, 0:128]
        ref[where + (slice(256 + window, 256 + 2 * window),)] = ds[:, view]
        ref[where + (slice(256 + 2 * window, 384 + 2 * window),)] = facts

    def tell_all():
        lane8 = lax.broadcasted_iota(jnp.int32, (8, 128), 1)
        power = jnp.sum(ds[...] * ds[...], axis=1, keepdims=True)
        facts = jnp.where(lane8 < 64, rho_ref[...], power)

        def tell(d):
            e = MEMBERS - 1 - d
            to, g = member(e)
            fill(gs, to[1], (e, slice(None)), facts)
            remote(gs.at[e], gb.at[mine], g_s, g_r, to).start()

        loop(0, peers, tell)
        fill(gb, label, (mine,), facts)

    def reduce_and_apply(par, first, last, index):
        publish_chunk, curves = publisher(par, first, last)
        for t in range(CHUNKS + LAG):
            if t < CHUNKS:
                scatter(t)
                if first and t == 0:
                    share_stats()
            c = t - FLIGHT
            if 0 <= c < CHUNKS:
                cross(c, par)
                if first and c == 0:
                    cross_stats()
                if first and c + 1 == CHUNKS:
                    loop(1, sets, lambda h: [copy.start() for copy in to_twin(h)])
            c = t - LAG
            if 0 <= c < CHUNKS:
                if first and c == 0:
                    start_state()
                publish_chunk(c)
        rescale(sum(curves[1:], curves[0]))
        for c in range(CHUNKS):
            pair(c).wait_send()
            total_wait(sbuf.at[c, pl.ds(1, peers)], rs_s.at[c], rs_r.at[c]).wait_send()
        if last:
            tell_all()
        slots = -(-CHUNKS // 2) if last else CHUNKS
        for slot in range(slots):
            gather(slot)
        total_wait(ab.at[pl.ds(0, peers * 8)], ab_s, ab_r).wait_recv()
        forward_ab().start()
        if not first:
            begin = (index - 1) * share
            loop(begin, jnp.minimum(begin + share, 2 * sets), tell_fellows)
        if groups > 1:
            for c in range(CHUNKS):
                total_wait(stbuf.at[par, c, pl.ds(0, groups - 1)], st_s.at[par, c], st_r.at[par, c]).wait_send()
        out = applied(slots, last)
        forward_ab().wait_recv()
        applied_z = cz[...] - ab[:, 0:1] * out
        cz[...] = applied_z
        inner[...] = applied_z + ab[:, 64:65] * inner[...]

    def begin_step(lhs, terms):
        for c in range(CHUNKS):
            product(lhs, terms, c)
            pair(c).start()

    local_stat, near_stat, member_stat, group_stat = 0, 1, 2, 2 + MEMBERS

    def pair_stats():
        return remote(stat.at[local_stat], stat.at[near_stat], sp_s, sp_r, partner)

    def share_stats():
        pair_stats().wait_recv()
        stat[member_stat + me] = stat[local_stat] + stat[near_stat]
        ref = stat.at[member_stat + me]
        loop(1, MEMBERS, lambda e: remote(ref, ref, sm_s, sm_r, member(e)[0]).start())

    def cross_stats():
        total_wait(stat.at[pl.ds(member_stat, peers)], sm_s, sm_r).wait_recv()
        acc = stat[member_stat]
        for e in range(1, MEMBERS):
            acc = acc + stat[member_stat + e]
        stat[group_stat + group] = acc
        ref = stat.at[group_stat + group]
        loop(1, groups, lambda h: remote(ref, ref, sg_s, sg_r, other(h)).start())

    def start_state():
        if groups > 1:
            total_wait(stat.at[pl.ds(group_stat, groups - 1)], sg_s, sg_r).wait_recv()
        acc = stat[group_stat]
        for h in range(1, groups):
            acc = acc + stat[group_stat + h]
        damping = damp_fraction * 2.0 * jnp.sum(
            jnp.sum(acc, axis=0, keepdims=True), axis=1, keepdims=True
        ) / (tokens * width)
        damp_ref[...] = jnp.broadcast_to(damping, damp_ref.shape)
        diag = scale * acc + damping
        inverse = 1.0 / diag
        for j in range(stat_rows):
            inv[:, j * 128 : (j + 1) * 128] = jnp.broadcast_to(inverse[j : j + 1, :], (8, 128))
        row = lax.broadcasted_iota(jnp.int32, (block, 128), 0)
        lane = lax.broadcasted_iota(jnp.int32, (block, 128), 1)
        every = jnp.sum(jnp.where(row == lane, diag[0:1, :], 0.0), axis=1, keepdims=True)
        row8 = lax.broadcasted_iota(jnp.int32, (8, 128), 0) + core * half + me * 8
        lane8 = lax.broadcasted_iota(jnp.int32, (8, 128), 1)
        unit = jnp.where(row8 == lane8, 1.0, 0.0)
        own_diag = jnp.sum(unit * diag[0:1, :], axis=1, keepdims=True)
        diag_ref[...] = own_diag
        rho_ref[...] = jnp.broadcast_to(1.0 / own_diag, (8, 128))
        rs[...] = jnp.zeros_like(rs)
        ds[...] = jnp.zeros_like(ds)
        xs[...] = jnp.zeros_like(xs)
        rs[:, 0:128] = unit
        ds[:, 0:128] = unit / own_diag
        scaled = cz[...] / every
        cz[...] = scaled
        inner[...] = scaled
        pair_stats().wait_send()
        total_wait(stat.at[pl.ds(member_stat, peers)], sm_s, sm_r).wait_send()
        if groups > 1:
            total_wait(stat.at[pl.ds(group_stat, groups - 1)], sg_s, sg_r).wait_send()

    share = -(-2 * sets // (steps - 1))

    def fetch(c):
        return pltpu.make_async_copy(calib_ref.at[:, lanes(c)], c_ref.at[:, lanes(c)], load.at[c])

    for c in range(CHUNKS):
        fetch(c).start()
    fetch_mask = pltpu.make_async_copy(m_ref, mask_ref, load.at[CHUNKS])
    fetch_weights = pltpu.make_async_copy(w_ref, wg_ref.at[label], load.at[CHUNKS + 1])
    fetch_mask.start()
    fetch_weights.start()
    one = jnp.where(
        lax.broadcasted_iota(jnp.int32, (block, 128), 0) == lax.broadcasted_iota(jnp.int32, (block, 128), 1), 1.0, 0.0
    )
    fetch(0).wait()
    turned = lax.dot_general(
        one.astype(jnp.bfloat16), c_ref[:, 0:block], (((1,), (1,)), ((), ())), preferred_element_type=f32
    )
    cz[...] = turned
    lhs = turned.astype(jnp.bfloat16)
    product(lhs, 1, 0)
    stat[local_stat] = jnp.zeros(stat.shape[1:], f32)
    for c in range(CHUNKS):
        if c:
            fetch(c).wait()
        for j in range(c * chunk // 128, (c + 1) * chunk // 128):
            square = c_ref[:, j * 128 : (j + 1) * 128].astype(f32)
            stat[local_stat, j : j + 1, :] = jnp.sum(square * square, axis=0, keepdims=True)
    pl.semaphore_wait(barrier, n)
    pair_stats().start()
    pair(0).start()
    for c in range(1, CHUNKS):
        product(lhs, 1, c)
        pair(c).start()
    fetch_mask.wait()
    mg_ref[columns(label)] = mask_ref[...].astype(f32).T.astype(jnp.bfloat16)
    fetch_weights.wait()
    reduce_and_apply(0, True, False, 0)
    loop(1, sets, lambda h: [copy.wait_recv() for copy in to_twin(h)])

    def iteration(index, carry):
        begin_step(two_terms(inner[...]), 2)
        finish_sends()
        reduce_and_apply(lax.rem(index, 2), False, False, index)
        return carry

    lax.fori_loop(1, steps - 1, iteration, 0)
    begin_step(two_terms(inner[...]), 2)
    finish_sends()
    reduce_and_apply((steps - 1) % 2, False, True, steps - 1)
    energy = inner[...]
    local_ref[...] = lax.dot_general(
        jnp.ones((8, energy.shape[1]), f32),
        energy * energy,
        (((1,), (1,)), ((), ())),
        precision=lax.Precision.HIGHEST,
        preferred_element_type=f32,
    )
    near = remote(local_ref, part, e_s, e_r, partner)
    near.start()
    near.wait_recv()
    slots[chip] = local_ref[...] + part[...]

    def far(d, j):
        return remote(slots.at[j], slots.at[j], en_s, en_r, chip_device(d))

    loop(1, n, lambda d: far(d, chip).start())
    finish_sends(-(-CHUNKS // 2))
    loop(1, sets, lambda h: [copy.wait_send() for copy in to_twin(h)])
    loop(0, 2 * sets, lambda t: [copy.wait_send() for copy in from_fellows(t)])
    loop(0, 2 * sets, lambda t: [copy.wait_recv() for copy in from_fellows(t)])
    total_wait(slots.at[pl.ds(0, n - 1)], en_s, en_r).wait_recv()
    norms = lax.fori_loop(1, n, lambda j, acc: acc + slots[j], slots[0])
    total_wait(gb.at[pl.ds(0, peers * 8)], g_s, g_r).wait_recv()
    last = remote(gb.at[half_rows], gb.at[half_rows], gf_s, gf_r, partner)
    last.start()
    near.wait_send()
    total_wait(slots.at[pl.ds(0, n - 1)], en_s, en_r).wait_send()
    total_wait(gs.at[pl.ds(1, peers)], g_s, g_r).wait_send()
    last.wait_recv()
    curve = scale * jnp.sum(one * norms[0:1, :], axis=1, keepdims=True)
    rho = gb[:, 256 + 2 * window : 257 + 2 * window]
    power = gb[:, 320 + 2 * window : 321 + 2 * window]
    alpha = rho / (curve + damp_ref[0:1, 0:1] * power)
    top_ref[...] = gb[:, 0:128] + alpha * gb[:, 128 + window : 256 + window]
    win_ref[...] = gb[:, 128 : 128 + window] + alpha * gb[:, 256 + window : 256 + 2 * window]
    last.wait_send()


def conjugate_gradients(calib, w, mask, block, cols, tokens, nd, nl):
    width = calib.shape[1]
    window = window_width(block, cols, nl)
    nx = math.isqrt(nl // 2)
    groups = (nx // 2) * (nd // 4) * (nl // nx // 2)
    sets = (nx // 2) * (nl // nx // 2)
    n = nd // 2 * nl
    chunk = width // CHUNKS
    f32, bf16 = jnp.float32, jnp.bfloat16
    vmem = pl.BlockSpec(memory_space=pltpu.VMEM)
    dma = pltpu.SemaphoreType.DMA
    stat_rows = -(-(width // 128) // 8) * 8
    message = 384 + 2 * window
    return pl.pallas_call(
        functools.partial(cg_kernel, nd, nl, cols, tokens),
        out_shape=(
            jax.ShapeDtypeStruct((block, 128), f32),
            jax.ShapeDtypeStruct((block, window), f32),
            jax.ShapeDtypeStruct((nl,) + w.shape, w.dtype),
            jax.ShapeDtypeStruct((block, mask.shape[0] * nl), bf16),
        ),
        in_specs=[pl.BlockSpec(memory_space=pltpu.HBM)] * 3,
        out_specs=(vmem,) * 4,
        scratch_shapes=[
            pltpu.VMEM(calib.shape, bf16),
            pltpu.VMEM(mask.shape, mask.dtype),
            pltpu.VMEM((CHUNKS, block, chunk), f32),
            pltpu.VMEM((CHUNKS, block // 2, chunk), f32),
            pltpu.VMEM((CHUNKS, MEMBERS, 8, chunk), f32),
            pltpu.VMEM((CHUNKS, MEMBERS, 8, chunk), f32),
            pltpu.VMEM((2, CHUNKS, groups, 8, chunk), f32),
            pltpu.VMEM((CHUNKS, 2 * block, chunk), bf16),
            pltpu.VMEM((block, 128), f32),
            pltpu.VMEM((8, width), f32),
            pltpu.VMEM((8, width), f32),
            pltpu.VMEM((8, width), f32),
            pltpu.VMEM((8, width), f32),
            pltpu.VMEM((8, width), f32),
            pltpu.VMEM((8, 128), f32),
            pltpu.VMEM((8, 1), f32),
            pltpu.VMEM((8, 128), f32),
            pltpu.VMEM((block, calib.shape[0]), f32),
            pltpu.VMEM((block, calib.shape[0]), f32),
            pltpu.VMEM((2 + MEMBERS + groups, stat_rows, 128), f32),
            pltpu.VMEM((MEMBERS, 8, message), f32),
            pltpu.VMEM((block, message), f32),
            pltpu.VMEM((8, block), f32),
            pltpu.VMEM((8, block), f32),
            pltpu.VMEM((n, 8, block), f32),
        ]
        + [dma((CHUNKS,))] * 4
        + [dma((2, CHUNKS))] * 2
        + [dma((CHUNKS,))] * 4
        + [dma] * 4
        + [dma] * 6
        + [dma] * 4
        + [dma] * 4
        + [dma((sets,))] * 4
        + [dma((2 * sets,))] * 4
        + [dma((CHUNKS + 2,))],
        compiler_params=pltpu.CompilerParams(collective_id=0, has_side_effects=True, vmem_limit_bytes=52 << 20),
        name="conjugate_gradients",
    )(calib, w, mask)


def finish_kernel(w_ref, m_ref, top_ref, t_ref, rest_ref, kept_ref, out_ref, sym, lower, tri, scales, errors, kept):
    block, rows = w_ref.shape
    own = kept_ref.shape[0]
    cols = rest_ref.shape[0]
    width = tri.shape[1]
    f32, bf16 = jnp.float32, jnp.bfloat16
    group = 512 if rows % 512 == 0 else rows
    top = top_ref[...]
    sym[...] = 0.5 * (top + top.T)
    lower[...] = jnp.zeros_like(lower)
    errors[...] = jnp.zeros_like(errors)
    tri[...] = jnp.zeros_like(tri)
    row = lax.broadcasted_iota(jnp.int32, (sub_width, 128), 0)

    def wide(x, lanes):
        return jnp.concatenate([x] * (lanes // 128), axis=1)

    def split(x):
        high = x.astype(bf16)
        return high, (x - high.astype(f32)).astype(bf16)

    for begin in range(0, block, sub_width):
        at = slice(begin, begin + sub_width)
        target = jnp.concatenate([sym[at, :], t_ref[at, :]], axis=1)
        if begin:
            factor = lower[...].T[at, :]
            target = target - jnp.dot(
                factor, tri[...], precision=lax.Precision.HIGHEST, preferred_element_type=f32
            )
            high, low = split(factor)
            factors = jnp.concatenate(
                [jnp.concatenate([high, high], axis=1), jnp.concatenate([low, jnp.zeros_like(low)], axis=1)], axis=0
            )
        spread = [
            jnp.broadcast_to(target[:, begin + j : begin + j + 1], (sub_width, 128)) for j in range(sub_width)
        ]
        steps = []
        inverses = []
        for j in range(sub_width):
            inverse = 1.0 / spread[j][j : j + 1, :]
            step = jnp.where(row > j, spread[j] * inverse, 0.0)
            for k in range(j + 1, sub_width):
                spread[k] = spread[k] - step * spread[k][j : j + 1, :]
            steps.append(step)
            inverses.append(inverse)
        for j in range(sub_width):
            target = target - wide(steps[j], width) * target[j : j + 1, :]
        tri[at, :] = target
        inverse = jnp.concatenate(inverses, axis=0)
        scales[at, :] = inverse
        lower[at, :] = target[:, :block] * inverse
        for first in range(0, rows, group):
            lanes = slice(first, first + group)
            window = w_ref[at, lanes].astype(f32)
            chosen = m_ref[at, lanes].astype(f32)
            if begin:
                both = jnp.dot(factors, errors[:, lanes], preferred_element_type=f32)
                window = window - (both[:sub_width] + both[sub_width:])
            for j in range(sub_width):
                window = window - wide(steps[j], group) * (chosen[j : j + 1, :] * window[j : j + 1, :])
            error = chosen * window
            high, low = split(error)
            errors[at, lanes] = high
            errors[slice(block + begin, block + begin + sub_width), lanes] = low
            kept[at, lanes] = window - error
    label = lax.axis_index("label")
    kept_ref[...] = kept[:, pl.ds(pl.multiple_of(label * own, 128), own)].T.astype(kept_ref.dtype)
    cross = (tri[:, 128:] * wide(scales[...], width - 128)).T[:cols]
    high, low = split(cross)
    twice = jnp.concatenate([high, high], axis=1)
    for first in range(0, rows, group):
        lanes = slice(first, first + group)
        delta = jnp.dot(twice, errors[:, lanes], preferred_element_type=f32)
        delta = delta + jnp.dot(low, errors[:block, lanes], preferred_element_type=f32)
        out_ref[:, lanes] = (rest_ref[:, lanes].astype(f32) - delta).astype(out_ref.dtype)


def finish(weights, mask, top, target, rest, own):
    block, rows = weights.shape
    cols = rest.shape[0]
    f32, bf16 = jnp.float32, jnp.bfloat16
    padded = -(-cols // 128) * 128
    target = jnp.pad(target, ((0, 0), (0, padded - cols)))
    vmem = pl.BlockSpec(memory_space=pltpu.VMEM)
    return pl.pallas_call(
        finish_kernel,
        out_shape=(jax.ShapeDtypeStruct((own, block), bf16), jax.ShapeDtypeStruct((cols, rows), bf16)),
        in_specs=[vmem] * 5,
        out_specs=(vmem, vmem),
        scratch_shapes=[
            pltpu.VMEM((block, block), f32),
            pltpu.VMEM((block, block), f32),
            pltpu.VMEM((block, 128 + padded), f32),
            pltpu.VMEM((block, 128), f32),
            pltpu.VMEM((2 * block, rows), bf16),
            pltpu.VMEM((block, rows), f32),
        ],
        compiler_params=pltpu.CompilerParams(vmem_limit_bytes=48 << 20),
        name="finish",
    )(weights, mask, top, target, rest)


def per_device(calib, block_weight, rest_weight, prune_mask):
    block = prune_mask.shape[1]
    nd, nl = lax.axis_size("dp"), lax.axis_size("label")
    own = prune_mask.shape[0]
    label = lax.axis_index("label")
    width = calib.shape[1]
    rest_cols = rest_weight.shape[1]
    top, near, weights, mask = conjugate_gradients(
        calib,
        block_weight.T,
        prune_mask,
        block,
        rest_cols,
        calib.shape[0] * nd * nl,
        nd,
        nl,
    )
    weights = weights.reshape(block, -1)
    begin = window_start(label, block, rest_cols, near.shape[1], width)
    owned = lax.dynamic_slice_in_dim(near, block + label * rest_cols - begin, rest_cols, 1)
    pruned_block, updated_rest = finish(weights, mask, top, owned, rest_weight.T, own)
    return (pruned_block, updated_rest.T)


def solution(mesh):
    return jax.shard_map(
        per_device,
        mesh=mesh,
        in_specs=(
            P(("dp", "label"), None),
            P("dp", "label"),
            P("dp", "label"),
            P(("dp", "label"), None),
        ),
        out_specs=(P(("dp", "label"), None), P("dp", "label")),
        check_vma=False,
    )
```
